32 devices in a mesh: lat: 8 (over z, core), lon: 4 (over y, x).
Axes of the slice: x: 2, y: 2, z: 4, core: 2. Of those that a mesh axis runs over, the one named last changes fastest.
Arguments:
- latent: float32 [64, 112, 640], P('lat', 'lon'), may hold values from -6 to 6
- conv_first: float32 [25, 640], replicated, may hold values from -1.2 to 1.2
- conv_second: float32 [25, 640], replicated, may hold values from -1.2 to 1.2
- filter_gains: float32 [48, 640], P(None, 'lon'), may hold values from -4 to 4
- norm_gain: float32 [640], replicated, may hold values from 0.5 to 1.5
- up_weight: bfloat16 [640, 1280], replicated, may hold values from -0.25 to 0.25
- down_weight: bfloat16 [1280, 640], replicated, may hold values from -0.15625 to 0.15625
Outputs:
- block_out: float32 [64, 112, 640], P('lat', 'lon')
The draws below stay inside these ranges and needn't reach their ends.
All inputs are finite; a program needn't handle non-finite values.
Results may differ from the reference program's by a relative error of at most 0.0012.
Values sent between devices are 32-bit elements; how exact they have to be, the bound alone decides.
A program may use at most 64 MiB of HBM per device.

```python
import jax
import jax.numpy as jnp
from jax import lax

C = 640
HIDDEN_SIZE = 1280
MODES = 48
NLAT = 64
NLON = 112


def steps_of(key, shape, pieces, low, top_value):
    def one(axis_at, blocks):
        steps = jax.random.uniform(jax.random.fold_in(jax.random.fold_in(key, 6), axis_at), (blocks,), jnp.float32, low / len(pieces), top_value / len(pieces))
        return jnp.repeat(jnp.exp(steps), shape[axis_at] // blocks).reshape((-1,) + (1,) * (len(shape) - axis_at - 1))

    gain = one(*pieces[0])
    for cut in pieces[1:]:
        gain = gain * one(*cut)
    return gain


def bell_draw(stream_key, dims, deviation, bound, pieces=(), kind=jnp.bfloat16):
    gain = steps_of(stream_key, dims, pieces, -0.22, 0.18) if pieces else 1.0
    values = jax.random.normal(stream_key, dims, jnp.float32) * deviation * gain
    return jnp.minimum(jnp.maximum(values, -bound), bound).astype(kind)


def setup_inputs(seed: int = 0) -> dict:
    key_of = jax.random.split(jax.random.key(seed), 8)
    return {
        "latent": bell_draw(key_of[0], (NLAT, NLON, C), 1.0, 6.0, ((0, 8), (1, 4)), jnp.float32),
        "conv_first": bell_draw(key_of[1], (25, C), 0.2, 1.2, (), jnp.float32),
        "conv_second": bell_draw(key_of[2], (25, C), 0.2, 1.2, (), jnp.float32),
        "filter_gains": bell_draw(key_of[3], (MODES, C), 1.0, 4.0, ((1, 4),), jnp.float32),
        "norm_gain": jnp.clip(1.0 + 0.1 * jax.random.normal(key_of[4], (C,), jnp.float32), 0.5, 1.5),
        "up_weight": bell_draw(key_of[5], (C, HIDDEN_SIZE), C ** -0.5, 0.25),
        "down_weight": bell_draw(key_of[6], (HIDDEN_SIZE, C), HIDDEN_SIZE ** -0.5, 0.15625),
    }


highest = lax.Precision.HIGHEST

def stencil_sum(padded, weights, row_count, col_count):
    stencil_total = jnp.zeros((row_count, col_count, padded.shape[2]), padded.dtype)
    for row_shift in range(5):
        for col_shift in range(5):
            stencil_total = stencil_total + weights[row_shift * 5 + col_shift] * padded[row_shift:row_shift + row_count, col_shift:col_shift + col_count, :]
    return stencil_total

def local_stencil(latent, weights):
    wrapped = jnp.concatenate([latent[:, -2:], latent, latent[:, :2]], axis=1)
    padded = jnp.pad(wrapped, ((2, 2), (0, 0), (0, 0)))
    return stencil_sum(padded, weights, latent.shape[0], latent.shape[1])

def colatitude(cell_count, float_type):
    cell_index = jnp.arange(cell_count).astype(jnp.int32).astype(float_type)
    return jnp.pi * (cell_index + 0.5) / cell_count

def legendre_table(orders, degrees, cosine, sine_theta):
    log_seed = 0.5 * (jnp.log((2.0 * orders + 1.0) / (4.0 * jnp.pi)) + jax.scipy.special.gammaln(2.0 * orders + 1.0) - 2.0 * orders * jnp.log(2.0) - 2.0 * jax.scipy.special.gammaln(orders + 1.0))
    diagonal_term = jnp.exp(log_seed[:, None] + orders[:, None] * jnp.log(sine_theta)[None, :])
    blanks = jnp.zeros_like(diagonal_term)
    legendre = jnp.zeros((orders.shape[0], degrees, sine_theta.shape[0]), diagonal_term.dtype)

    def block_step(block_index, state_tuple):
        previous, earlier, legendre = state_tuple
        values = []
        for offset in range(8):
            degree = (block_index * 8 + offset).astype(diagonal_term.dtype)
            square = degree * degree
            upper_ratio = jnp.sqrt(jnp.maximum(4.0 * square - 1.0, 1.0) / jnp.maximum(square - orders * orders, 1.0))
            below_sq = (degree - 1.0) * (degree - 1.0)
            lower_ratio = jnp.sqrt(jnp.maximum(below_sq - orders * orders, 0.0) / jnp.maximum(4.0 * below_sq - 1.0, 1.0))
            recurred = upper_ratio[:, None] * (cosine[None, :] * previous - lower_ratio[:, None] * earlier)
            current = jnp.where((degree < orders)[:, None], blanks, jnp.where((degree == orders)[:, None], diagonal_term, recurred))
            values.append(current)
            earlier = previous
            previous = current
        stacked = jnp.stack(values, axis=1)
        legendre = lax.dynamic_update_slice(legendre, stacked, (jnp.int32(0), (block_index * 8).astype(jnp.int32), jnp.int32(0)))
        return (previous, earlier, legendre)
    return lax.fori_loop(0, degrees // 8, block_step, (blanks, blanks, legendre))[2]

def fourier_tables(lon_count, mode_count, float_type):
    product_index = jnp.arange(lon_count).astype(jnp.int32)[:, None] * jnp.arange(mode_count).astype(jnp.int32)[None, :] % lon_count
    phase_grid = 2.0 * jnp.pi * product_index.astype(float_type) / lon_count
    forward = jnp.stack([jnp.cos(phase_grid), -jnp.sin(phase_grid)], axis=1) / lon_count
    factor = jnp.where(jnp.arange(mode_count).astype(jnp.int32) == 0, 1.0, 2.0).astype(float_type)
    inverse = jnp.stack([jnp.cos(phase_grid).T * factor[:, None], -jnp.sin(phase_grid).T * factor[:, None]], axis=0)
    return (forward, inverse)

def harmonic_filter(latent, filter_gains):
    lat_count, lon_count = (latent.shape[0], latent.shape[1])
    mode_count = filter_gains.shape[0]
    forward, inverse = fourier_tables(lon_count, mode_count, jnp.float32)
    colat_grid = colatitude(lat_count, jnp.float32)
    orders = jnp.arange(mode_count).astype(jnp.int32).astype(jnp.float32)
    legendre = legendre_table(orders, mode_count, jnp.cos(colat_grid), jnp.sin(colat_grid))
    quadrature = 2.0 * jnp.pi * jnp.pi * jnp.sin(colat_grid) / lat_count
    weighted = legendre * quadrature
    coeffs = jnp.einsum('inc,nrk->irkc', latent, forward, precision=highest)
    spectrum = jnp.einsum('kli,irkc->lrkc', weighted, coeffs, precision=highest)
    spectrum = spectrum * filter_gains[:, None, None, :]
    restored = jnp.einsum('kli,lrkc->irkc', legendre, spectrum, precision=highest)
    return jnp.einsum('irkc,rkn->inc', restored, inverse, precision=highest)

def channel_mlp(latent, norm_gain, up_weight, down_weight):
    average = lax.optimization_barrier(jnp.mean(latent, axis=-1, keepdims=True))
    centred = latent - average
    spread = lax.optimization_barrier(jnp.mean(centred * centred, axis=-1, keepdims=True))
    normed = (centred * lax.rsqrt(spread + 1e-05) * norm_gain).astype(jnp.bfloat16)
    hidden = jnp.dot(normed, up_weight, preferred_element_type=jnp.float32)
    active = jax.nn.gelu(hidden, approximate=True).astype(jnp.bfloat16)
    return latent + jnp.dot(active, down_weight, preferred_element_type=jnp.float32)

def reference(latent, conv_first, conv_second, filter_gains, norm_gain, up_weight, down_weight):
    after_first = latent + local_stencil(latent, conv_first)
    after_second = after_first + harmonic_filter(after_first, filter_gains)
    after_third = after_second + local_stencil(after_second, conv_second)
    return channel_mlp(after_third, norm_gain, up_weight, down_weight)
```

```python
import functools
import math

import jax
import jax.numpy as jnp
import numpy as np
from jax import lax
from jax.experimental import pallas as pl
from jax.experimental.pallas import tpu as pltpu
from jax.sharding import PartitionSpec as P

highest = lax.Precision.HIGHEST


def padded_2(block, sides, width):
    for axis, dim in sides:
        count = lax.axis_size(axis)
        forward = [(i, i + 1) for i in range(count - 1)]
        backward = [(target, source) for source, target in forward]
        low = lax.ppermute(
            lax.slice_in_dim(block, block.shape[dim] - width, None, axis=dim), axis, forward
        )
        high = lax.ppermute(lax.slice_in_dim(block, 0, width, axis=dim), axis, backward)
        block = jnp.concatenate([low, block, high], axis=dim)
    return block


def stencil_sum(padded, weights, row_count, col_count):
    stencil_total = jnp.zeros((row_count, col_count, padded.shape[2]), padded.dtype)
    for row_shift in range(5):
        for col_shift in range(5):
            stencil_total = (
                stencil_total
                + weights[row_shift * 5 + col_shift]
                * padded[row_shift : row_shift + row_count, col_shift : col_shift + col_count, :]
            )
    return stencil_total


def slice_stencil(sliced, weights):
    lat_extended = padded_2(sliced, (("lat", 0),), 2)
    wrapped = jnp.concatenate([lat_extended[:, -2:], lat_extended, lat_extended[:, :2]], axis=1)
    return stencil_sum(wrapped, weights, sliced.shape[0], sliced.shape[1])


def colatitude(cell_count, float_type):
    cell_index = jnp.arange(cell_count).astype(float_type)
    return jnp.pi * (cell_index + 0.5) / cell_count


def legendre_table(orders, degrees, cosine, sine_theta):
    log_seed = 0.5 * (
        jnp.log((2.0 * orders + 1.0) / (4.0 * jnp.pi))
        + jax.scipy.special.gammaln(2.0 * orders + 1.0)
        - 2.0 * orders * jnp.log(2.0)
        - 2.0 * jax.scipy.special.gammaln(orders + 1.0)
    )
    diagonal_term = jnp.exp(log_seed[:, None] + orders[:, None] * jnp.log(sine_theta)[None, :])
    blanks = jnp.zeros_like(diagonal_term)
    legendre = jnp.zeros((orders.shape[0], degrees, sine_theta.shape[0]), diagonal_term.dtype)

    def block_step(block_index, state_tuple):
        previous, earlier, legendre = state_tuple
        values = []
        for offset in range(8):
            degree = (block_index * 8 + offset).astype(diagonal_term.dtype)
            square = degree * degree
            upper_ratio = jnp.sqrt(
                jnp.maximum(4.0 * square - 1.0, 1.0) / jnp.maximum(square - orders * orders, 1.0)
            )
            below_sq = (degree - 1.0) * (degree - 1.0)
            lower_ratio = jnp.sqrt(
                jnp.maximum(below_sq - orders * orders, 0.0)
                / jnp.maximum(4.0 * below_sq - 1.0, 1.0)
            )
            recurred = upper_ratio[:, None] * (
                cosine[None, :] * previous - lower_ratio[:, None] * earlier
            )
            current = jnp.where(
                (degree < orders)[:, None],
                blanks,
                jnp.where((degree == orders)[:, None], diagonal_term, recurred),
            )
            values.append(current)
            earlier = previous
            previous = current
        stacked = jnp.stack(values, axis=1)
        legendre = lax.dynamic_update_slice(
            legendre, stacked, (jnp.int32(0), (block_index * 8).astype(jnp.int32), jnp.int32(0))
        )
        return (previous, earlier, legendre)

    return lax.fori_loop(0, degrees // 8, block_step, (blanks, blanks, legendre))[2]


def fourier_tables(lon_count, mode_count, float_type):
    product_index = jnp.arange(lon_count)[:, None] * jnp.arange(mode_count)[None, :] % lon_count
    phase_grid = 2.0 * jnp.pi * product_index.astype(float_type) / lon_count
    forward = jnp.stack([jnp.cos(phase_grid), -jnp.sin(phase_grid)], axis=1) / lon_count
    factor = jnp.where(jnp.arange(mode_count) == 0, 1.0, 2.0).astype(float_type)
    inverse = jnp.stack(
        [jnp.cos(phase_grid).T * factor[:, None], -jnp.sin(phase_grid).T * factor[:, None]], axis=0
    )
    return (forward, inverse)


def channel_mlp(latent, norm_gain, up_weight, down_weight):
    average = jnp.mean(latent, axis=-1, keepdims=True)
    centred = latent - average
    spread = jnp.mean(centred * centred, axis=-1, keepdims=True)
    normed = (centred * lax.rsqrt(spread + 1e-05) * norm_gain).astype(jnp.bfloat16)
    hidden = jnp.dot(normed, up_weight, preferred_element_type=jnp.float32)
    active = jax.nn.gelu(hidden, approximate=True).astype(jnp.bfloat16)
    return latent + jnp.dot(active, down_weight, preferred_element_type=jnp.float32)


def per_device(latent, conv_first, conv_second, filter_gains, norm_gain, up_weight, down_weight):
    lat_size = lax.axis_size("lat")
    lon_size = lax.axis_size("lon")
    lat_local = latent.shape[0]
    lon_local = latent.shape[1]
    slice_width = filter_gains.shape[1]
    mode_count = filter_gains.shape[0]
    lat_count = lat_local * lat_size
    lon_count = lon_local * lon_size
    order_count = mode_count // lat_size
    channel_start = lax.axis_index("lon") * slice_width
    sliced = lax.all_to_all(latent, "lon", split_axis=2, concat_axis=1, tiled=True)
    first_taps = lax.dynamic_slice_in_dim(conv_first, channel_start, slice_width, 1)
    first_sliced = sliced + slice_stencil(sliced, first_taps)
    forward, inverse = fourier_tables(lon_count, mode_count, jnp.float32)
    colat_grid = colatitude(lat_count, jnp.float32)
    orders = (lax.axis_index("lat") * order_count + jnp.arange(order_count)).astype(jnp.float32)
    legendre = legendre_table(orders, mode_count, jnp.cos(colat_grid), jnp.sin(colat_grid))
    quadrature = 2.0 * jnp.pi * jnp.pi * jnp.sin(colat_grid) / lat_count
    weighted = legendre * quadrature
    coeffs = jnp.einsum("inc,nrk->irkc", first_sliced, forward, precision=highest)
    spectrum = jnp.einsum(
        "kli,irkc->lrkc",
        weighted,
        lax.all_to_all(coeffs, "lat", split_axis=2, concat_axis=0, tiled=True),
        precision=highest,
    )
    spectrum = spectrum * filter_gains[:, None, None, :]
    restored = jnp.einsum("kli,lrkc->irkc", legendre, spectrum, precision=highest)
    returned = lax.all_to_all(restored, "lat", split_axis=0, concat_axis=2, tiled=True)
    filtered = jnp.einsum("irkc,rkn->inc", returned, inverse, precision=highest)
    second_taps = lax.dynamic_slice_in_dim(conv_second, channel_start, slice_width, 1)
    second_sliced = first_sliced + filtered
    incoming = second_sliced + slice_stencil(second_sliced, second_taps)
    arrived = lax.all_to_all(incoming, "lon", split_axis=1, concat_axis=2, tiled=True)
    return channel_mlp(arrived, norm_gain, up_weight, down_weight)


LANES = 128
TILE = 8
bf16 = jnp.bfloat16
f32 = jnp.float32


def legendre_numpy(modes, lat_count):
    theta = np.pi * (np.arange(lat_count) + 0.5) / lat_count
    cosine, sine = np.cos(theta), np.sin(theta)
    table = np.zeros((modes, modes, lat_count))
    for m in range(modes):
        seed = 0.5 * (
            math.log((2 * m + 1) / (4 * math.pi))
            + math.lgamma(2 * m + 1)
            - 2 * m * math.log(2.0)
            - 2 * math.lgamma(m + 1)
        )
        table[m, m] = np.exp(seed + m * np.log(sine))
        for l in range(m + 1, modes):
            a = math.sqrt((4.0 * l * l - 1) / (l * l - m * m))
            b = math.sqrt(max((l - 1.0) ** 2 - m * m, 0.0) / (4.0 * (l - 1.0) ** 2 - 1)) if l > 1 else 0.0
            earlier = table[m, l - 2] if l > m + 1 else 0.0
            table[m, l] = a * (cosine * table[m, l - 1] - b * earlier)
    quadrature = 2 * np.pi**2 * sine / lat_count
    return table, table * quadrature


def split_numpy(table):
    high = table.astype(np.float32).astype(jnp.bfloat16)
    low = (table - high.astype(np.float64)).astype(np.float32).astype(jnp.bfloat16)
    return np.stack([high, low])


@functools.lru_cache(maxsize=None)
def constant_tables(nl, nj, rows, cols, modes):
    lat_count, lon_count = rows * nl, cols * nj
    rs = rows // nj
    pair = TILE // rs // 2
    groups = modes // nl // pair
    n = np.arange(lon_count)
    k = np.arange(modes)
    phase = 2 * np.pi * ((k[:, None] * n[None, :]) % lon_count) / lon_count
    trig = np.stack([np.cos(phase), -np.sin(phase)], axis=1)
    factor = np.where(k == 0, 1.0, 2.0)
    same = np.eye(rs)
    by_order = trig.reshape(nl, groups, pair, 2, lon_count)
    forward = by_order.reshape(nl, groups, pair, 2, nj, cols) / lon_count
    forward = np.einsum("lqopjn,rs->lqropjsn", forward, same)
    forward = forward.reshape(modes * 2 * rs, nj * rs * cols)
    wide = cols + 4
    where = (np.arange(nj)[:, None] * cols + np.arange(wide)[None, :] - 2) % lon_count
    back = (trig * factor[:, None, None]).reshape(nl, groups, pair, 2, lon_count)[..., where]
    back = np.einsum("lqopjn,rs->jrnlqsop", back, same)
    back = back.reshape(nj * rs * wide, modes * 2 * rs)
    pick = np.zeros((nj, wide, lon_count))
    pick[np.arange(nj)[:, None], np.arange(wide)[None, :], where] = 1.0
    pick = np.einsum("jwtn,rs->jrwtsn", pick.reshape(nj, wide, nj, cols), same)
    pick = pick.reshape(nj * rs * wide, nj * rs * cols)
    table, weighted = legendre_numpy(modes, lat_count)

    def by_lat(values):
        parts = split_numpy(values)
        parts = parts.reshape((2, nl, modes // nl) + values.shape[1:])
        return np.moveaxis(parts, 1, 0)

    return (
        split_numpy(forward),
        split_numpy(back),
        pick.astype(jnp.bfloat16),
        by_lat(weighted),
        by_lat(np.swapaxes(table, 1, 2)),
    )


def halves(value):
    high = value.astype(bf16)
    return high, (value - high.astype(f32)).astype(bf16)


def mm(a, b):
    return jnp.dot(a, b, preferred_element_type=f32)


def mm3(a_high, a_low, b):
    high, low = halves(b)
    return mm(a_high, high) + (mm(a_high, low) + mm(a_low, high))


def stencil_block(source, taps, cols, rows, width):
    totals = [None] * rows
    for r in range(rows + 4):
        base = source[r, :, cols]
        for b in range(5):
            moved = base if b == 0 else pltpu.roll(base, base.shape[0] - b, 0)
            for a in range(5):
                i = r - a
                if 0 <= i < rows:
                    term = taps[a * 5 + b : a * 5 + b + 1, cols] * moved
                    if a == 2 and b == 2:
                        term = term + moved
                    totals[i] = term if totals[i] is None else totals[i] + term
    return [total[:width] for total in totals]


def block_kernel(
    nl, nj,
    latent, taps1, taps2, gains, norm_gain, fwd, back, pick, up_hbm, down_hbm, wt_hbm, pt_hbm,
    out,
    row_in, west_out, east_out, west_in, east_in, first_pad, mine, circle, sent_c, spec_in,
    spec_out, got_c, wide_out, second_pad, gain_in, gain_all, third, up, down, wt, pt,
    load_sem, row_s, row_r, col_s, col_r, gain_s, gain_r, a_s, a_r, c_s, c_r, b_s, b_r, z_s, z_r,
    halo_s, halo_r,
):
    rows, cols, channels = latent.shape
    wide = cols + 4
    blocks = channels // LANES
    rs = rows // nj
    part = rs * cols
    total = nl * nj
    per = spec_in.shape[0]
    orders = wt.shape[1]
    pair = TILE // rs // 2
    groups = orders // pair
    units = groups * blocks
    lat_count = rows * nl
    la, lo = lax.axis_index("lat"), lax.axis_index("lon")
    me = la * nj + lo
    above, below = lax.rem(la + nl - 1, nl), lax.rem(la + 1, nl)
    right, left = lax.rem(lo + 1, nj), lax.rem(lo + nj - 1, nj)
    has_above, has_below = la > 0, la < nl - 1

    def span(start, size):
        return pl.ds(start if isinstance(start, int) else pl.multiple_of(start, TILE), size)

    def lanes(block):
        return pl.ds(block * LANES, LANES)

    def rcopy(src, dst, send, recv, a, b):
        return pltpu.make_async_remote_copy(
            src_ref=src, dst_ref=dst, send_sem=send, recv_sem=recv,
            device_id={"lat": a, "lon": b}, device_id_type=pl.DeviceIdType.MESH,
        )

    loads = [
        pltpu.make_async_copy(wt_hbm.at[la], wt, load_sem.at[0]),
        pltpu.make_async_copy(pt_hbm.at[la], pt, load_sem.at[1]),
        pltpu.make_async_copy(up_hbm, up, load_sem.at[2]),
        pltpu.make_async_copy(down_hbm, down, load_sem.at[3]),
    ]
    for load in loads:
        load.start()

    barrier = pltpu.get_barrier_semaphore()

    def greet(d, carry):
        peer = lax.rem(me + d, total)
        pl.semaphore_signal(
            barrier, inc=1, device_id={"lat": peer // nj, "lon": lax.rem(peer, nj)},
            device_id_type=pl.DeviceIdType.MESH,
        )
        return carry

    lax.fori_loop(1, total, greet, 0)
    for i in range(rows):
        west_out[i] = latent[i, 0:2, :]
        east_out[i] = latent[i, cols - 2 : cols, :]
    pl.semaphore_wait(barrier, total - 1)

    halos = [
        (has_below, has_above,
         rcopy(latent.at[pl.ds(rows - 2, 2)], row_in.at[0], row_s.at[0], row_r.at[0], below, lo)),
        (has_above, has_below,
         rcopy(latent.at[pl.ds(0, 2)], row_in.at[1], row_s.at[1], row_r.at[1], above, lo)),
    ]
    for side, (source, target, to) in enumerate(((east_out, west_in, right), (west_out, east_in, left))):
        s, r = col_s.at[side], col_r.at[side]
        halos += [
            (None, None, rcopy(source, target.at[pl.ds(2, rows)], s.at[0], r.at[0], la, to)),
            (has_below, has_above,
             rcopy(source.at[pl.ds(rows - 2, 2)], target.at[pl.ds(0, 2)], s.at[1], r.at[1], below, to)),
            (has_above, has_below,
             rcopy(source.at[pl.ds(0, 2)], target.at[pl.ds(rows + 2, 2)], s.at[2], r.at[2], above, to)),
        ]

    def guarded(guard, action):
        if guard is None:
            action()
        else:
            pl.when(guard)(action)

    for send, _, copy in halos:
        guarded(send, copy.start)
    gain_copies = []
    for d in range(1, nj):
        gain_copies.append(
            rcopy(gains, gain_in.at[lo], gain_s.at[d], gain_r.at[d], la, lax.rem(lo + d, nj))
        )
    for copy in gain_copies:
        copy.start()
    gain_in[lo] = gains[...]
    first_pad[2 : rows + 2, 2 : cols + 2, :] = latent[...]
    blank = jnp.zeros((2, wide, channels), f32)
    for absent, place in ((la == 0, pl.ds(0, 2)), (la == nl - 1, pl.ds(rows + 2, 2))):
        @pl.when(absent)
        def _(place=place):
            first_pad[place] = blank
            second_pad[place] = blank
    for _, arrive, copy in halos:
        guarded(arrive, copy.wait_recv)
    for side, (guard, base) in enumerate(((has_above, 0), (has_below, rows + 2))):
        @pl.when(guard)
        def _(side=side, base=base):
            for i in range(2):
                first_pad[base + i, 2 : cols + 2, :] = row_in[side, i]
                first_pad[base + i, 0:2, :] = west_in[base + i]
                first_pad[base + i, cols + 2 : wide, :] = east_in[base + i]
    for i in range(rows):
        first_pad[2 + i, 0:2, :] = west_in[2 + i]
        first_pad[2 + i, cols + 2 : wide, :] = east_in[2 + i]

    def a_copy(block, d):
        to = lax.rem(lo + d, nj)
        return rcopy(
            mine.at[span(to * part, part), lanes(block)], circle.at[lo, :, lanes(block)],
            a_s.at[block, d], a_r.at[block, d], la, to,
        )

    def z_copy(block, d):
        to = lax.rem(lo + d, nj)
        return rcopy(
            wide_out.at[pl.ds(to * rs, rs), :, lanes(block)],
            second_pad.at[pl.ds(2 + lo * rs, rs), :, lanes(block)],
            z_s.at[block, d], z_r.at[block, d], la, to,
        )

    def c_copy(a, b):
        peer = a * nj + b
        return rcopy(
            sent_c.at[a, pl.ds(per * b, per)], spec_in.at[:, span(me * TILE, TILE), :],
            c_s.at[peer], c_r.at[me], a, b,
        )

    def c_arrival(peer, a, b):
        return rcopy(
            sent_c.at[a, pl.ds(per * b, per)], spec_in.at[:, span(peer * TILE, TILE), :],
            c_s.at[peer], c_r.at[peer], a, b,
        )

    def b_copy(a, b):
        peer = a * nj + b
        return rcopy(
            spec_out.at[:, span(peer * TILE, TILE), :], got_c.at[la, pl.ds(per * lo, per)],
            b_s.at[peer], b_r.at[me], a, b,
        )

    def b_arrival(peer, a, b):
        return rcopy(
            spec_out.at[:, span(peer * TILE, TILE), :], got_c.at[a, pl.ds(per * b, per)],
            b_s.at[peer], b_r.at[peer], a, b,
        )

    for block in range(blocks):
        sums = stencil_block(first_pad, taps1, lanes(block), rows, cols)
        for i in range(rows):
            mine[cols * i : cols * (i + 1), lanes(block)] = sums[i][:cols]
        for d in range(1, nj):
            a_copy(block, d).start()
        circle[lo, :, lanes(block)] = mine[span(lo * part, part), lanes(block)]

    if per * nj > units:
        sent_c[:, units:] = jnp.zeros((nl, per * nj - units, TILE, LANES), f32)
    for block in range(blocks):
        for d in range(1, nj):
            a_copy(block, d).wait_recv()
        values = circle[:, :, lanes(block)].reshape(nj * part, LANES)
        coeffs = mm3(fwd[0], fwd[1], values)
        sent_c[:, block * groups : (block + 1) * groups] = coeffs.reshape(nl, groups, TILE, LANES)
        for b in range(nj):
            if (min(per * (b + 1), units) - 1) // groups == block:
                def send_lat(d, carry, b=b):
                    a = lax.rem(la + d, nl)

                    @pl.when(a * nj + b != me)
                    def _():
                        c_copy(a, b).start()
                    return carry

                lax.fori_loop(0, nl, send_lat, 0)

    spec_in[:, span(me * TILE, TILE), :] = sent_c[la, pl.ds(per * lo, per)]
    for copy in gain_copies:
        copy.wait_recv()
    width = gains.shape[1]
    for j in range(nj):
        gain_all[:, width * j : width * (j + 1)] = gain_in[j]
    loads[0].wait()
    loads[1].wait()

    def take_c(peer, carry):
        @pl.when(peer != me)
        def _():
            c_arrival(peer, peer // nj, lax.rem(peer, nj)).wait_recv()
        return carry

    lax.fori_loop(0, total, take_c, 0)

    for t in range(per):
        unit = per * lo + t
        block = jnp.minimum(unit // groups, blocks - 1)
        group = lax.rem(unit, groups)
        gain = gain_all[:, pl.ds(pl.multiple_of(block * LANES, LANES), LANES)]
        gain = jnp.concatenate([gain, gain], axis=1)
        for o in range(pair):
            data = jnp.concatenate(
                [spec_in[t, pl.ds(2 * o + ri, lat_count, stride=2 * pair), :] for ri in range(2)], axis=1
            )
            order = group * pair + o
            spectrum = mm3(wt[0, order], wt[1, order], data) * gain
            restored = mm3(pt[0, order], pt[1, order], spectrum)
            for ri in range(2):
                spec_out[t, pl.ds(2 * o + ri, lat_count, stride=2 * pair), :] = (
                    restored[:, ri * LANES : (ri + 1) * LANES]
                )

    def send_b(d, carry):
        peer = lax.rem(me + d, total)
        b_copy(peer // nj, lax.rem(peer, nj)).start()
        return carry

    lax.fori_loop(1, total, send_b, 0)
    got_c[la, pl.ds(per * lo, per)] = spec_out[:, span(me * TILE, TILE), :]

    taken = set()
    for block in range(blocks):
        for unit in range(block * groups, (block + 1) * groups):
            b = unit // per
            if b not in taken:
                taken.add(b)

                def take_b(a, carry, b=b):
                    @pl.when(a * nj + b != me)
                    def _():
                        b_arrival(a * nj + b, a, b).wait_recv()
                    return carry

                lax.fori_loop(0, nl, take_b, 0)
        coeffs = got_c[:, block * groups : (block + 1) * groups].reshape(nl * groups * TILE, LANES)
        values = circle[:, :, lanes(block)].reshape(nj * part, LANES)
        high, low = halves(values)
        rebuilt = mm3(back[0], back[1], coeffs) + (mm(pick[...], low) + mm(pick[...], high))
        wide_out[:, :, lanes(block)] = rebuilt.reshape(nj * rs, wide, LANES)
        for d in range(1, nj):
            z_copy(block, d).start()
        second_pad[pl.ds(2 + lo * rs, rs), :, lanes(block)] = wide_out[pl.ds(lo * rs, rs), :, lanes(block)]

    def row_copies(block):
        edge = second_pad.at[:, :, lanes(block)]
        return (
            (has_below, has_above,
             rcopy(edge.at[pl.ds(rows, 2)], edge.at[pl.ds(0, 2)], halo_s.at[block, 0], halo_r.at[block, 0], below, lo)),
            (has_above, has_below,
             rcopy(edge.at[pl.ds(2, 2)], edge.at[pl.ds(rows + 2, 2)], halo_s.at[block, 1], halo_r.at[block, 1], above, lo)),
        )

    for block in range(blocks):
        for d in range(1, nj):
            z_copy(block, d).wait_recv()
        for send, _, copy in row_copies(block):
            guarded(send, copy.start)
    for block in range(blocks):
        for _, arrive, copy in row_copies(block):
            guarded(arrive, copy.wait_recv)
        sums = stencil_block(second_pad, taps2, lanes(block), rows, cols)
        for i in range(rows):
            third[cols * i : cols * (i + 1), lanes(block)] = sums[i][:cols]

    loads[2].wait()
    loads[3].wait()
    state = third[...]
    average = jnp.mean(state, axis=-1, keepdims=True)
    centred = state - average
    spread = jnp.mean(centred * centred, axis=-1, keepdims=True)
    normed = (centred * lax.rsqrt(spread + 1e-05) * norm_gain[...]).astype(bf16)
    active = jax.nn.gelu(mm(normed, up[...]), approximate=True).astype(bf16)
    third[...] = state + mm(active, down[...])
    for i in range(rows):
        out[i] = third[cols * i : cols * (i + 1), :]

    for send, _, copy in halos:
        guarded(send, copy.wait_send)
    for copy in gain_copies:
        copy.wait_send()
    for block in range(blocks):
        for d in range(1, nj):
            a_copy(block, d).wait_send()
            z_copy(block, d).wait_send()
        for send, _, copy in row_copies(block):
            guarded(send, copy.wait_send)

    def finish(peer, carry):
        @pl.when(peer != me)
        def _():
            a, b = peer // nj, lax.rem(peer, nj)
            c_copy(a, b).wait_send()
            b_copy(a, b).wait_send()
        return carry

    lax.fori_loop(0, total, finish, 0)


def fused(nl, nj, latent, conv_first, conv_second, filter_gains, norm_gain, up_weight, down_weight):
    rows, cols, channels = latent.shape
    modes, width = filter_gains.shape
    forward, back, pick, wt, pt = (jnp.asarray(t) for t in constant_tables(nl, nj, rows, cols, modes))
    rs = rows // nj
    wide = cols + 4
    blocks = channels // LANES
    total = nl * nj
    groups = modes // nl // (TILE // rs // 2)
    per = -(-groups * blocks // nj)
    vm = lambda *shape, kind=f32: pltpu.VMEM(shape, kind)
    dma = lambda *shape: pltpu.SemaphoreType.DMA(shape)
    here = pl.BlockSpec(memory_space=pltpu.VMEM)
    far = pl.BlockSpec(memory_space=pltpu.HBM)
    return pl.pallas_call(
        functools.partial(block_kernel, nl, nj),
        out_shape=jax.ShapeDtypeStruct(latent.shape, f32),
        in_specs=[here] * 8 + [far] * 4,
        out_specs=here,
        scratch_shapes=[
            vm(2, 2, cols, channels),
            vm(rows, 2, channels),
            vm(rows, 2, channels),
            vm(rows + 4, 2, channels),
            vm(rows + 4, 2, channels),
            vm(rows + 4, wide, channels),
            vm(rows * cols, channels),
            vm(nj, rs * cols, channels),
            vm(nl, per * nj, TILE, LANES),
            vm(per, total * TILE, LANES),
            vm(per, total * TILE, LANES),
            vm(nl, per * nj, TILE, LANES),
            vm(nj * rs, wide, channels),
            vm(rows + 4, wide, channels),
            vm(nj, modes, width),
            vm(modes, channels),
            vm(rows * cols, channels),
            vm(*up_weight.shape, kind=bf16),
            vm(*down_weight.shape, kind=bf16),
            vm(*wt.shape[1:], kind=bf16),
            vm(*pt.shape[1:], kind=bf16),
            dma(4),
            dma(2), dma(2), dma(2, 3), dma(2, 3), dma(nj), dma(nj),
            dma(blocks, nj), dma(blocks, nj), dma(total), dma(total), dma(total), dma(total),
            dma(blocks, nj), dma(blocks, nj), dma(blocks, 2), dma(blocks, 2),
        ],
        compiler_params=pltpu.CompilerParams(
            collective_id=0, has_side_effects=True, vmem_limit_bytes=60 * 1024 * 1024
        ),
        name="block",
    )(
        latent, conv_first, conv_second, filter_gains, norm_gain[None, :], forward, back, pick,
        up_weight, down_weight, wt, pt,
    )


def fits(nl, nj, latent, filter_gains):
    rows, cols, channels = latent.shape
    modes = filter_gains.shape[0]
    if rows % nj or channels % LANES or modes % nl or nj < 2 or nl < 2:
        return False
    rs = rows // nj
    if TILE % (2 * rs) or (rs * cols) % TILE or (cols + 4) % TILE:
        return False
    return (modes // nl) % (TILE // rs // 2) == 0


def body(latent, conv_first, conv_second, filter_gains, norm_gain, up_weight, down_weight):
    nl, nj = lax.axis_size("lat"), lax.axis_size("lon")
    arguments = (latent, conv_first, conv_second, filter_gains, norm_gain, up_weight, down_weight)
    if fits(nl, nj, latent, filter_gains):
        return fused(nl, nj, *arguments)
    return per_device(*arguments)


def solution(mesh):
    return jax.shard_map(
        body,
        mesh=mesh,
        in_specs=(P("lat", "lon", None), P(), P(), P(None, "lon"), P(), P(), P()),
        out_specs=P("lat", "lon", None),
        check_vma=False,
    )
```

```python
import functools
import math

import jax
import jax.numpy as jnp
import numpy as np
from jax import lax
from jax.experimental import pallas as pl
from jax.experimental.pallas import tpu as pltpu
from jax.sharding import PartitionSpec as P

highest = lax.Precision.HIGHEST


def padded_2(block, sides, width):
    for axis, dim in sides:
        count = lax.axis_size(axis)
        forward = [(i, i + 1) for i in range(count - 1)]
        backward = [(target, source) for source, target in forward]
        low = lax.ppermute(
            lax.slice_in_dim(block, block.shape[dim] - width, None, axis=dim), axis, forward
        )
        high = lax.ppermute(lax.slice_in_dim(block, 0, width, axis=dim), axis, backward)
        block = jnp.concatenate([low, block, high], axis=dim)
    return block


def stencil_sum(padded, weights, row_count, col_count):
    stencil_total = jnp.zeros((row_count, col_count, padded.shape[2]), padded.dtype)
    for row_shift in range(5):
        for col_shift in range(5):
            stencil_total = (
                stencil_total
                + weights[row_shift * 5 + col_shift]
                * padded[row_shift : row_shift + row_count, col_shift : col_shift + col_count, :]
            )
    return stencil_total


def slice_stencil(sliced, weights):
    lat_extended = padded_2(sliced, (("lat", 0),), 2)
    wrapped = jnp.concatenate([lat_extended[:, -2:], lat_extended, lat_extended[:, :2]], axis=1)
    return stencil_sum(wrapped, weights, sliced.shape[0], sliced.shape[1])


def colatitude(cell_count, float_type):
    cell_index = jnp.arange(cell_count).astype(float_type)
    return jnp.pi * (cell_index + 0.5) / cell_count


def legendre_table(orders, degrees, cosine, sine_theta):
    log_seed = 0.5 * (
        jnp.log((2.0 * orders + 1.0) / (4.0 * jnp.pi))
        + jax.scipy.special.gammaln(2.0 * orders + 1.0)
        - 2.0 * orders * jnp.log(2.0)
        - 2.0 * jax.scipy.special.gammaln(orders + 1.0)
    )
    diagonal_term = jnp.exp(log_seed[:, None] + orders[:, None] * jnp.log(sine_theta)[None, :])
    blanks = jnp.zeros_like(diagonal_term)
    legendre = jnp.zeros((orders.shape[0], degrees, sine_theta.shape[0]), diagonal_term.dtype)

    def block_step(block_index, state_tuple):
        previous, earlier, legendre = state_tuple
        values = []
        for offset in range(8):
            degree = (block_index * 8 + offset).astype(diagonal_term.dtype)
            square = degree * degree
            upper_ratio = jnp.sqrt(
                jnp.maximum(4.0 * square - 1.0, 1.0) / jnp.maximum(square - orders * orders, 1.0)
            )
            below_sq = (degree - 1.0) * (degree - 1.0)
            lower_ratio = jnp.sqrt(
                jnp.maximum(below_sq - orders * orders, 0.0)
                / jnp.maximum(4.0 * below_sq - 1.0, 1.0)
            )
            recurred = upper_ratio[:, None] * (
                cosine[None, :] * previous - lower_ratio[:, None] * earlier
            )
            current = jnp.where(
                (degree < orders)[:, None],
                blanks,
                jnp.where((degree == orders)[:, None], diagonal_term, recurred),
            )
            values.append(current)
            earlier = previous
            previous = current
        stacked = jnp.stack(values, axis=1)
        legendre = lax.dynamic_update_slice(
            legendre, stacked, (jnp.int32(0), (block_index * 8).astype(jnp.int32), jnp.int32(0))
        )
        return (previous, earlier, legendre)

    return lax.fori_loop(0, degrees // 8, block_step, (blanks, blanks, legendre))[2]


def fourier_tables(lon_count, mode_count, float_type):
    product_index = jnp.arange(lon_count)[:, None] * jnp.arange(mode_count)[None, :] % lon_count
    phase_grid = 2.0 * jnp.pi * product_index.astype(float_type) / lon_count
    forward = jnp.stack([jnp.cos(phase_grid), -jnp.sin(phase_grid)], axis=1) / lon_count
    factor = jnp.where(jnp.arange(mode_count) == 0, 1.0, 2.0).astype(float_type)
    inverse = jnp.stack(
        [jnp.cos(phase_grid).T * factor[:, None], -jnp.sin(phase_grid).T * factor[:, None]], axis=0
    )
    return (forward, inverse)


def channel_mlp(latent, norm_gain, up_weight, down_weight):
    average = jnp.mean(latent, axis=-1, keepdims=True)
    centred = latent - average
    spread = jnp.mean(centred * centred, axis=-1, keepdims=True)
    normed = (centred * lax.rsqrt(spread + 1e-05) * norm_gain).astype(jnp.bfloat16)
    hidden = jnp.dot(normed, up_weight, preferred_element_type=jnp.float32)
    active = jax.nn.gelu(hidden, approximate=True).astype(jnp.bfloat16)
    return latent + jnp.dot(active, down_weight, preferred_element_type=jnp.float32)


def per_device(latent, conv_first, conv_second, filter_gains, norm_gain, up_weight, down_weight):
    lat_size = lax.axis_size("lat")
    lon_size = lax.axis_size("lon")
    lat_local = latent.shape[0]
    lon_local = latent.shape[1]
    slice_width = filter_gains.shape[1]
    mode_count = filter_gains.shape[0]
    lat_count = lat_local * lat_size
    lon_count = lon_local * lon_size
    order_count = mode_count // lat_size
    channel_start = lax.axis_index("lon") * slice_width
    sliced = lax.all_to_all(latent, "lon", split_axis=2, concat_axis=1, tiled=True)
    first_taps = lax.dynamic_slice_in_dim(conv_first, channel_start, slice_width, 1)
    first_sliced = sliced + slice_stencil(sliced, first_taps)
    forward, inverse = fourier_tables(lon_count, mode_count, jnp.float32)
    colat_grid = colatitude(lat_count, jnp.float32)
    orders = (lax.axis_index("lat") * order_count + jnp.arange(order_count)).astype(jnp.float32)
    legendre = legendre_table(orders, mode_count, jnp.cos(colat_grid), jnp.sin(colat_grid))
    quadrature = 2.0 * jnp.pi * jnp.pi * jnp.sin(colat_grid) / lat_count
    weighted = legendre * quadrature
    coeffs = jnp.einsum("inc,nrk->irkc", first_sliced, forward, precision=highest)
    spectrum = jnp.einsum(
        "kli,irkc->lrkc",
        weighted,
        lax.all_to_all(coeffs, "lat", split_axis=2, concat_axis=0, tiled=True),
        precision=highest,
    )
    spectrum = spectrum * filter_gains[:, None, None, :]
    restored = jnp.einsum("kli,lrkc->irkc", legendre, spectrum, precision=highest)
    returned = lax.all_to_all(restored, "lat", split_axis=0, concat_axis=2, tiled=True)
    filtered = jnp.einsum("irkc,rkn->inc", returned, inverse, precision=highest)
    second_taps = lax.dynamic_slice_in_dim(conv_second, channel_start, slice_width, 1)
    second_sliced = first_sliced + filtered
    incoming = second_sliced + slice_stencil(second_sliced, second_taps)
    arrived = lax.all_to_all(incoming, "lon", split_axis=1, concat_axis=2, tiled=True)
    return channel_mlp(arrived, norm_gain, up_weight, down_weight)


LANES = 128
TILE = 8
bf16 = jnp.bfloat16
f32 = jnp.float32


def legendre_numpy(modes, lat_count):
    theta = np.pi * (np.arange(lat_count) + 0.5) / lat_count
    cosine, sine = np.cos(theta), np.sin(theta)
    table = np.zeros((modes, modes, lat_count))
    for m in range(modes):
        seed = 0.5 * (
            math.log((2 * m + 1) / (4 * math.pi))
            + math.lgamma(2 * m + 1)
            - 2 * m * math.log(2.0)
            - 2 * math.lgamma(m + 1)
        )
        table[m, m] = np.exp(seed + m * np.log(sine))
        for l in range(m + 1, modes):
            a = math.sqrt((4.0 * l * l - 1) / (l * l - m * m))
            b = math.sqrt(max((l - 1.0) ** 2 - m * m, 0.0) / (4.0 * (l - 1.0) ** 2 - 1)) if l > 1 else 0.0
            earlier = table[m, l - 2] if l > m + 1 else 0.0
            table[m, l] = a * (cosine * table[m, l - 1] - b * earlier)
    quadrature = 2 * np.pi**2 * sine / lat_count
    return table, table * quadrature


def split_numpy(table):
    high = table.astype(np.float32).astype(jnp.bfloat16)
    low = (table - high.astype(np.float64)).astype(np.float32).astype(jnp.bfloat16)
    return np.stack([high, low])


@functools.lru_cache(maxsize=None)
def constant_tables(nl, nj, rows, cols, modes):
    lat_count, lon_count = rows * nl, cols * nj
    rs = rows // nj
    pair = TILE // rs // 2
    groups = modes // nl // pair
    n = np.arange(lon_count)
    k = np.arange(modes)
    phase = 2 * np.pi * ((k[:, None] * n[None, :]) % lon_count) / lon_count
    trig = np.stack([np.cos(phase), -np.sin(phase)], axis=1)
    factor = np.where(k == 0, 1.0, 2.0)
    same = np.eye(rs)
    by_order = trig.reshape(nl, groups, pair, 2, lon_count)
    forward = by_order.reshape(nl, groups, pair, 2, nj, cols) / lon_count
    forward = np.einsum("lqopjn,rs->lqropjsn", forward, same)
    forward = forward.reshape(modes * 2 * rs, nj * rs * cols)
    wide = cols + 4
    where = (np.arange(nj)[:, None] * cols + np.arange(wide)[None, :] - 2) % lon_count
    back = (trig * factor[:, None, None]).reshape(nl, groups, pair, 2, lon_count)[..., where]
    back = np.einsum("lqopjn,rs->jrnlqsop", back, same)
    back = back.reshape(nj * rs * wide, modes * 2 * rs)
    pick = np.zeros((nj, wide, lon_count))
    pick[np.arange(nj)[:, None], np.arange(wide)[None, :], where] = 1.0
    pick = np.einsum("jwtn,rs->jrwtsn", pick.reshape(nj, wide, nj, cols), same)
    pick = pick.reshape(nj * rs * wide, nj * rs * cols)
    table, weighted = legendre_numpy(modes, lat_count)

    def by_lat(values):
        room = -values.shape[2] % (LANES // 2)
        parts = split_numpy(np.pad(values, ((0, 0), (0, 0), (0, room))))
        parts = np.concatenate([parts[0], parts[1]], axis=-1)
        return parts.reshape((nl, modes // nl) + parts.shape[1:])

    return (
        split_numpy(forward),
        split_numpy(back),
        pick.astype(jnp.bfloat16),
        by_lat(weighted),
        by_lat(np.swapaxes(table, 1, 2)),
    )


def halves(value):
    high = value.astype(bf16)
    return high, (value - high.astype(f32)).astype(bf16)


def mm(a, b):
    return jnp.dot(a, b, preferred_element_type=f32)


def mm3(a_high, a_low, b):
    high, low = halves(b)
    return mm(a_high, high) + (mm(a_high, low) + mm(a_low, high))


def mm_packed(table, value):
    depth = table.shape[1] // 2
    if value.shape[0] < depth:
        blank = jnp.zeros((depth - value.shape[0], value.shape[1]), f32)
        value = jnp.concatenate([value, blank], axis=0)
    high, low = halves(value)
    return mm(
        jnp.concatenate([table, table[:, :depth]], axis=1),
        jnp.concatenate([high, high, low], axis=0),
    )


def stencil_block(source, taps, cols, rows, width):
    totals = [None] * rows
    for r in range(rows + 4):
        base = source[r, :, cols]
        for b in range(5):
            moved = base if b == 0 else pltpu.roll(base, base.shape[0] - b, 0)
            for a in range(5):
                i = r - a
                if 0 <= i < rows:
                    term = taps[a * 5 + b : a * 5 + b + 1, cols] * moved
                    if a == 2 and b == 2:
                        term = term + moved
                    totals[i] = term if totals[i] is None else totals[i] + term
    return [total[:width] for total in totals]


def block_kernel(
    nl, nj, rows,
    latent, taps1, taps2, gains, norm_gain, fwd, back, pick, up_hbm, down_hbm, wt_hbm, pt_hbm,
    out,
    grid, row_out, row_in, west_out, east_out, west_in, east_in, first_pad, mine, circle, sent_c, spec_in,
    spec_out, got_c, wide_out, second_pad, gain_in, gain_all, third, up, down, wt, pt,
    load_sem, in_sem, out_sem, row_s, row_r, col_s, col_r, gain_s, gain_r, a_s, a_r, c_s, c_r, b_s, b_r, z_s, z_r,
    halo_s, halo_r,
):
    channels = latent.shape[1]
    cols = latent.shape[0] // rows
    wide = cols + 4
    blocks = channels // LANES
    rs = rows // nj
    part = rs * cols
    total = nl * nj
    per = spec_in.shape[0]
    orders = wt.shape[0]
    pair = TILE // rs // 2
    groups = orders // pair
    units = groups * blocks
    lat_count = rows * nl
    la, lo = lax.axis_index("lat"), lax.axis_index("lon")
    me = la * nj + lo
    above, below = lax.rem(la + nl - 1, nl), lax.rem(la + 1, nl)
    right, left = lax.rem(lo + 1, nj), lax.rem(lo + nj - 1, nj)
    has_above, has_below = la > 0, la < nl - 1

    def span(start, size):
        return pl.ds(start if isinstance(start, int) else pl.multiple_of(start, TILE), size)

    def lanes(block):
        return pl.ds(block * LANES, LANES)

    def rcopy(src, dst, send, recv, a, b):
        return pltpu.make_async_remote_copy(
            src_ref=src, dst_ref=dst, send_sem=send, recv_sem=recv,
            device_id={"lat": a, "lon": b}, device_id_type=pl.DeviceIdType.MESH,
        )

    loads = [
        pltpu.make_async_copy(wt_hbm.at[la], wt, load_sem.at[0]),
        pltpu.make_async_copy(pt_hbm.at[la], pt, load_sem.at[1]),
        pltpu.make_async_copy(up_hbm, up, load_sem.at[2]),
        pltpu.make_async_copy(down_hbm, down, load_sem.at[3]),
    ]

    def in_copy(block):
        return pltpu.make_async_copy(latent.at[:, lanes(block)], grid.at[block], in_sem.at[block])

    def out_copy(block):
        return pltpu.make_async_copy(grid.at[block], out.at[:, lanes(block)], out_sem.at[block])

    for block in range(blocks):
        in_copy(block).start()
    for load in loads:
        load.start()

    barrier = pltpu.get_barrier_semaphore()

    def greet(d, carry):
        peer = lax.rem(me + d, total)
        pl.semaphore_signal(
            barrier, inc=1, device_id={"lat": peer // nj, "lon": lax.rem(peer, nj)},
            device_id_type=pl.DeviceIdType.MESH,
        )
        return carry

    lax.fori_loop(1, total, greet, 0)
    for block in range(blocks):
        in_copy(block).wait()
        for i in range(rows):
            line = grid[block, pl.ds(i, cols, stride=rows), :]
            first_pad[2 + i, 2 : cols + 2, lanes(block)] = line
            west_out[i, :, lanes(block)] = line[:2]
            east_out[i, :, lanes(block)] = line[cols - 2 :]
            if i < 2:
                row_out[1, i, :, lanes(block)] = line
            if i >= rows - 2:
                row_out[0, i - rows + 2, :, lanes(block)] = line
    blank = jnp.zeros((2, wide, channels), f32)
    for absent, place in ((la == 0, pl.ds(0, 2)), (la == nl - 1, pl.ds(rows + 2, 2))):
        @pl.when(absent)
        def _(place=place):
            first_pad[place] = blank
            second_pad[place] = blank
    pl.semaphore_wait(barrier, total - 1)

    halos = [
        (has_below, has_above,
         rcopy(row_out.at[0], row_in.at[0], row_s.at[0], row_r.at[0], below, lo)),
        (has_above, has_below,
         rcopy(row_out.at[1], row_in.at[1], row_s.at[1], row_r.at[1], above, lo)),
    ]
    for side, (source, target, to) in enumerate(((east_out, west_in, right), (west_out, east_in, left))):
        s, r = col_s.at[side], col_r.at[side]
        halos += [
            (None, None, rcopy(source, target.at[pl.ds(2, rows)], s.at[0], r.at[0], la, to)),
            (has_below, has_above,
             rcopy(source.at[pl.ds(rows - 2, 2)], target.at[pl.ds(0, 2)], s.at[1], r.at[1], below, to)),
            (has_above, has_below,
             rcopy(source.at[pl.ds(0, 2)], target.at[pl.ds(rows + 2, 2)], s.at[2], r.at[2], above, to)),
        ]

    def guarded(guard, action):
        if guard is None:
            action()
        else:
            pl.when(guard)(action)

    for send, _, copy in halos:
        guarded(send, copy.start)
    gain_copies = []
    for d in range(1, nj):
        gain_copies.append(
            rcopy(gains, gain_in.at[lo], gain_s.at[d], gain_r.at[d], la, lax.rem(lo + d, nj))
        )
    for copy in gain_copies:
        copy.start()
    gain_in[lo] = gains[...]
    for _, arrive, copy in halos:
        guarded(arrive, copy.wait_recv)
    for side, (guard, base) in enumerate(((has_above, 0), (has_below, rows + 2))):
        @pl.when(guard)
        def _(side=side, base=base):
            for i in range(2):
                first_pad[base + i, 2 : cols + 2, :] = row_in[side, i]
                first_pad[base + i, 0:2, :] = west_in[base + i]
                first_pad[base + i, cols + 2 : wide, :] = east_in[base + i]
    for i in range(rows):
        first_pad[2 + i, 0:2, :] = west_in[2 + i]
        first_pad[2 + i, cols + 2 : wide, :] = east_in[2 + i]

    def a_copy(block, d):
        to = lax.rem(lo + d, nj)
        return rcopy(
            mine.at[span(to * part, part), lanes(block)], circle.at[lo, :, lanes(block)],
            a_s.at[block, d], a_r.at[block, d], la, to,
        )

    def z_copy(block, d):
        to = lax.rem(lo + d, nj)
        return rcopy(
            wide_out.at[pl.ds(to * rs, rs), :, lanes(block)],
            second_pad.at[pl.ds(2 + lo * rs, rs), :, lanes(block)],
            z_s.at[block, d], z_r.at[block, d], la, to,
        )

    def c_copy(t, a, b, source):
        return rcopy(
            sent_c.at[a, nj * t + b], spec_in.at[t, span(source * TILE, TILE), :],
            c_s.at[t, a * nj + b], c_r.at[t, source], a, b,
        )

    def b_copy(t, a, b, la, lo):
        peer = a * nj + b
        return rcopy(
            spec_out.at[t, span(peer * TILE, TILE), :], got_c.at[la, nj * t + lo],
            b_s.at[t, peer], b_r.at[t, la * nj + lo], a, b,
        )

    def keep_c(t):
        spec_in[t, span(me * TILE, TILE), :] = sent_c[la, nj * t + lo]

    def others(action):
        def step(d, carry):
            peer = lax.rem(me + d, total)
            action(peer, peer // nj, lax.rem(peer, nj))
            return carry

        lax.fori_loop(1, total, step, 0)

    def own_unit(t, action):
        if nj * t + nj <= units:
            action()
        else:
            pl.when(nj * t + lo < units)(action)

    def real_unit(t, b, action):
        if nj * t + nj <= units:
            action()
        else:
            pl.when(nj * t + b < units)(action)

    for block in range(blocks):
        sums = stencil_block(first_pad, taps1, lanes(block), rows, cols)
        for i in range(rows):
            mine[cols * i : cols * (i + 1), lanes(block)] = sums[i][:cols]
        for d in range(1, nj):
            a_copy(block, d).start()
        circle[lo, :, lanes(block)] = mine[span(lo * part, part), lanes(block)]

    for block in range(blocks):
        for d in range(1, nj):
            a_copy(block, d).wait_recv()
        values = circle[:, :, lanes(block)].reshape(nj * part, LANES)
        coeffs = mm3(fwd[0], fwd[1], values)
        sent_c[:, block * groups : (block + 1) * groups] = coeffs.reshape(nl, groups, TILE, LANES)
        for t in range(per):
            if (min(nj * (t + 1), units) - 1) // groups == block:
                others(lambda peer, a, b, t=t: real_unit(t, b, c_copy(t, a, b, me).start))
                own_unit(t, lambda t=t: keep_c(t))

    for copy in gain_copies:
        copy.wait_recv()
    width = gains.shape[1]
    for j in range(nj):
        gain_all[:, width * j : width * (j + 1)] = gain_in[j]
    loads[0].wait()
    loads[1].wait()

    def filter_unit(t):
        others(lambda peer, a, b: c_copy(t, la, lo, peer).wait_recv())
        unit = nj * t + lo
        block = unit // groups
        group = lax.rem(unit, groups)
        gain = gain_all[:, pl.ds(pl.multiple_of(block * LANES, LANES), LANES)]
        gain = jnp.concatenate([gain, gain], axis=1)
        for o in range(pair):
            data = jnp.concatenate(
                [spec_in[t, pl.ds(2 * o + ri, lat_count, stride=2 * pair), :] for ri in range(2)], axis=1
            )
            order = group * pair + o
            restored = mm_packed(pt[order], mm_packed(wt[order], data) * gain)
            for ri in range(2):
                spec_out[t, pl.ds(2 * o + ri, lat_count, stride=2 * pair), :] = (
                    restored[:, ri * LANES : (ri + 1) * LANES]
                )
        others(lambda peer, a, b: b_copy(t, a, b, la, lo).start())
        got_c[la, nj * t + lo] = spec_out[t, span(me * TILE, TILE), :]

    for t in range(per):
        own_unit(t, lambda t=t: filter_unit(t))

    taken = set()
    for block in range(blocks):
        for unit in range(block * groups, (block + 1) * groups):
            t = unit // nj
            if t not in taken:
                taken.add(t)
                others(lambda peer, a, b, t=t: real_unit(t, b, b_copy(t, la, lo, a, b).wait_recv))
        coeffs = got_c[:, block * groups : (block + 1) * groups].reshape(nl * groups * TILE, LANES)
        values = circle[:, :, lanes(block)].reshape(nj * part, LANES)
        high, low = halves(values)
        rebuilt = mm3(back[0], back[1], coeffs) + (mm(pick[...], low) + mm(pick[...], high))
        wide_out[:, :, lanes(block)] = rebuilt.reshape(nj * rs, wide, LANES)
        for d in range(1, nj):
            z_copy(block, d).start()
        second_pad[pl.ds(2 + lo * rs, rs), :, lanes(block)] = wide_out[pl.ds(lo * rs, rs), :, lanes(block)]

    def row_copies(block):
        edge = second_pad.at[:, :, lanes(block)]
        return (
            (has_below, has_above,
             rcopy(edge.at[pl.ds(rows, 2)], edge.at[pl.ds(0, 2)], halo_s.at[block, 0], halo_r.at[block, 0], below, lo)),
            (has_above, has_below,
             rcopy(edge.at[pl.ds(2, 2)], edge.at[pl.ds(rows + 2, 2)], halo_s.at[block, 1], halo_r.at[block, 1], above, lo)),
        )

    for block in range(blocks):
        for d in range(1, nj):
            z_copy(block, d).wait_recv()
        for send, _, copy in row_copies(block):
            guarded(send, copy.start)
    for block in range(blocks):
        for _, arrive, copy in row_copies(block):
            guarded(arrive, copy.wait_recv)
        sums = stencil_block(second_pad, taps2, lanes(block), rows, cols)
        for i in range(rows):
            third[cols * i : cols * (i + 1), lanes(block)] = sums[i][:cols]

    loads[2].wait()
    loads[3].wait()
    state = third[...]
    average = jnp.mean(state, axis=-1, keepdims=True)
    centred = state - average
    spread = jnp.mean(centred * centred, axis=-1, keepdims=True)
    normed = (centred * lax.rsqrt(spread + 1e-05) * norm_gain[...].reshape(1, channels)).astype(bf16)
    active = jax.nn.gelu(mm(normed, up[...]), approximate=True).astype(bf16)
    third[...] = state + mm(active, down[...])
    for block in range(blocks):
        for i in range(rows):
            grid[block, pl.ds(i, cols, stride=rows), :] = third[cols * i : cols * (i + 1), lanes(block)]
        out_copy(block).start()

    for block in range(blocks):
        out_copy(block).wait()
    for send, _, copy in halos:
        guarded(send, copy.wait_send)
    for copy in gain_copies:
        copy.wait_send()
    for block in range(blocks):
        for d in range(1, nj):
            a_copy(block, d).wait_send()
            z_copy(block, d).wait_send()
        for send, _, copy in row_copies(block):
            guarded(send, copy.wait_send)

    for t in range(per):
        others(lambda peer, a, b, t=t: real_unit(t, b, c_copy(t, a, b, me).wait_send))
        own_unit(t, lambda t=t: others(lambda peer, a, b: b_copy(t, a, b, la, lo).wait_send()))


def fused(nl, nj, latent, conv_first, conv_second, filter_gains, norm_gain, up_weight, down_weight):
    rows, cols, channels = latent.shape
    modes, width = filter_gains.shape
    forward, back, pick, wt, pt = (jnp.asarray(t) for t in constant_tables(nl, nj, rows, cols, modes))
    rs = rows // nj
    wide = cols + 4
    blocks = channels // LANES
    total = nl * nj
    groups = modes // nl // (TILE // rs // 2)
    per = -(-groups * blocks // nj)
    vm = lambda *shape, kind=f32: pltpu.VMEM(shape, kind)
    dma = lambda *shape: pltpu.SemaphoreType.DMA(shape)
    here = pl.BlockSpec(memory_space=pltpu.VMEM)
    far = pl.BlockSpec(memory_space=pltpu.HBM)
    result = pl.pallas_call(
        functools.partial(block_kernel, nl, nj, rows),
        out_shape=jax.ShapeDtypeStruct((cols * rows, channels), f32),
        in_specs=[far] + [here] * 7 + [far] * 4,
        out_specs=far,
        scratch_shapes=[
            vm(blocks, cols * rows, LANES),
            vm(2, 2, cols, channels),
            vm(2, 2, cols, channels),
            vm(rows, 2, channels),
            vm(rows, 2, channels),
            vm(rows + 4, 2, channels),
            vm(rows + 4, 2, channels),
            vm(rows + 4, wide, channels),
            vm(rows * cols, channels),
            vm(nj, rs * cols, channels),
            vm(nl, per * nj, TILE, LANES),
            vm(per, total * TILE, LANES),
            vm(per, total * TILE, LANES),
            vm(nl, per * nj, TILE, LANES),
            vm(nj * rs, wide, channels),
            vm(rows + 4, wide, channels),
            vm(nj, modes, width),
            vm(modes, channels),
            vm(rows * cols, channels),
            vm(*up_weight.shape, kind=bf16),
            vm(*down_weight.shape, kind=bf16),
            vm(*wt.shape[1:], kind=bf16),
            vm(*pt.shape[1:], kind=bf16),
            dma(4), dma(blocks), dma(blocks),
            dma(2), dma(2), dma(2, 3), dma(2, 3), dma(nj), dma(nj),
            dma(blocks, nj), dma(blocks, nj), dma(per, total), dma(per, total), dma(per, total), dma(per, total),
            dma(blocks, nj), dma(blocks, nj), dma(blocks, 2), dma(blocks, 2),
        ],
        compiler_params=pltpu.CompilerParams(
            collective_id=0, has_side_effects=True, vmem_limit_bytes=60 * 1024 * 1024
        ),
        name="block",
    )(
        jnp.swapaxes(latent, 0, 1).reshape(cols * rows, channels), conv_first, conv_second,
        filter_gains, norm_gain, forward, back, pick, up_weight, down_weight, wt, pt,
    )
    return jnp.swapaxes(result.reshape(cols, rows, channels), 0, 1)


def fits(nl, nj, latent, filter_gains):
    rows, cols, channels = latent.shape
    modes = filter_gains.shape[0]
    if rows % nj or channels % LANES or modes % nl or nj < 2 or nl < 2:
        return False
    rs = rows // nj
    if TILE % (2 * rs) or (rs * cols) % TILE or (cols + 4) % TILE:
        return False
    if modes > LANES // 2 or rows * nl > LANES // 2:
        return False
    return (modes // nl) % (TILE // rs // 2) == 0


def body(latent, conv_first, conv_second, filter_gains, norm_gain, up_weight, down_weight):
    nl, nj = lax.axis_size("lat"), lax.axis_size("lon")
    arguments = (latent, conv_first, conv_second, filter_gains, norm_gain, up_weight, down_weight)
    if fits(nl, nj, latent, filter_gains):
        return fused(nl, nj, *arguments)
    return per_device(*arguments)


def solution(mesh):
    return jax.shard_map(
        body,
        mesh=mesh,
        in_specs=(P("lat", "lon", None), P(), P(), P(None, "lon"), P(), P(), P()),
        out_specs=P("lat", "lon", None),
        check_vma=False,
    )
```

```python
import functools
import math

import jax
import jax.numpy as jnp
import numpy as np
from jax import lax
from jax.experimental import pallas as pl
from jax.experimental.pallas import tpu as pltpu
from jax.sharding import PartitionSpec as P

highest = lax.Precision.HIGHEST


def padded_2(block, sides, width):
    for axis, dim in sides:
        count = lax.axis_size(axis)
        forward = [(i, i + 1) for i in range(count - 1)]
        backward = [(target, source) for source, target in forward]
        low = lax.ppermute(
            lax.slice_in_dim(block, block.shape[dim] - width, None, axis=dim), axis, forward
        )
        high = lax.ppermute(lax.slice_in_dim(block, 0, width, axis=dim), axis, backward)
        block = jnp.concatenate([low, block, high], axis=dim)
    return block


def stencil_sum(padded, weights, row_count, col_count):
    stencil_total = jnp.zeros((row_count, col_count, padded.shape[2]), padded.dtype)
    for row_shift in range(5):
        for col_shift in range(5):
            stencil_total = (
                stencil_total
                + weights[row_shift * 5 + col_shift]
                * padded[row_shift : row_shift + row_count, col_shift : col_shift + col_count, :]
            )
    return stencil_total


def slice_stencil(sliced, weights):
    lat_extended = padded_2(sliced, (("lat", 0),), 2)
    wrapped = jnp.concatenate([lat_extended[:, -2:], lat_extended, lat_extended[:, :2]], axis=1)
    return stencil_sum(wrapped, weights, sliced.shape[0], sliced.shape[1])


def colatitude(cell_count, float_type):
    cell_index = jnp.arange(cell_count).astype(float_type)
    return jnp.pi * (cell_index + 0.5) / cell_count


def legendre_table(orders, degrees, cosine, sine_theta):
    log_seed = 0.5 * (
        jnp.log((2.0 * orders + 1.0) / (4.0 * jnp.pi))
        + jax.scipy.special.gammaln(2.0 * orders + 1.0)
        - 2.0 * orders * jnp.log(2.0)
        - 2.0 * jax.scipy.special.gammaln(orders + 1.0)
    )
    diagonal_term = jnp.exp(log_seed[:, None] + orders[:, None] * jnp.log(sine_theta)[None, :])
    blanks = jnp.zeros_like(diagonal_term)
    legendre = jnp.zeros((orders.shape[0], degrees, sine_theta.shape[0]), diagonal_term.dtype)

    def block_step(block_index, state_tuple):
        previous, earlier, legendre = state_tuple
        values = []
        for offset in range(8):
            degree = (block_index * 8 + offset).astype(diagonal_term.dtype)
            square = degree * degree
            upper_ratio = jnp.sqrt(
                jnp.maximum(4.0 * square - 1.0, 1.0) / jnp.maximum(square - orders * orders, 1.0)
            )
            below_sq = (degree - 1.0) * (degree - 1.0)
            lower_ratio = jnp.sqrt(
                jnp.maximum(below_sq - orders * orders, 0.0)
                / jnp.maximum(4.0 * below_sq - 1.0, 1.0)
            )
            recurred = upper_ratio[:, None] * (
                cosine[None, :] * previous - lower_ratio[:, None] * earlier
            )
            current = jnp.where(
                (degree < orders)[:, None],
                blanks,
                jnp.where((degree == orders)[:, None], diagonal_term, recurred),
            )
            values.append(current)
            earlier = previous
            previous = current
        stacked = jnp.stack(values, axis=1)
        legendre = lax.dynamic_update_slice(
            legendre, stacked, (jnp.int32(0), (block_index * 8).astype(jnp.int32), jnp.int32(0))
        )
        return (previous, earlier, legendre)

    return lax.fori_loop(0, degrees // 8, block_step, (blanks, blanks, legendre))[2]


def fourier_tables(lon_count, mode_count, float_type):
    product_index = jnp.arange(lon_count)[:, None] * jnp.arange(mode_count)[None, :] % lon_count
    phase_grid = 2.0 * jnp.pi * product_index.astype(float_type) / lon_count
    forward = jnp.stack([jnp.cos(phase_grid), -jnp.sin(phase_grid)], axis=1) / lon_count
    factor = jnp.where(jnp.arange(mode_count) == 0, 1.0, 2.0).astype(float_type)
    inverse = jnp.stack(
        [jnp.cos(phase_grid).T * factor[:, None], -jnp.sin(phase_grid).T * factor[:, None]], axis=0
    )
    return (forward, inverse)


def channel_mlp(latent, norm_gain, up_weight, down_weight):
    average = jnp.mean(latent, axis=-1, keepdims=True)
    centred = latent - average
    spread = jnp.mean(centred * centred, axis=-1, keepdims=True)
    normed = (centred * lax.rsqrt(spread + 1e-05) * norm_gain).astype(jnp.bfloat16)
    hidden = jnp.dot(normed, up_weight, preferred_element_type=jnp.float32)
    active = jax.nn.gelu(hidden, approximate=True).astype(jnp.bfloat16)
    return latent + jnp.dot(active, down_weight, preferred_element_type=jnp.float32)


def per_device(latent, conv_first, conv_second, filter_gains, norm_gain, up_weight, down_weight):
    lat_size = lax.axis_size("lat")
    lon_size = lax.axis_size("lon")
    lat_local = latent.shape[0]
    lon_local = latent.shape[1]
    slice_width = filter_gains.shape[1]
    mode_count = filter_gains.shape[0]
    lat_count = lat_local * lat_size
    lon_count = lon_local * lon_size
    order_count = mode_count // lat_size
    channel_start = lax.axis_index("lon") * slice_width
    sliced = lax.all_to_all(latent, "lon", split_axis=2, concat_axis=1, tiled=True)
    first_taps = lax.dynamic_slice_in_dim(conv_first, channel_start, slice_width, 1)
    first_sliced = sliced + slice_stencil(sliced, first_taps)
    forward, inverse = fourier_tables(lon_count, mode_count, jnp.float32)
    colat_grid = colatitude(lat_count, jnp.float32)
    orders = (lax.axis_index("lat") * order_count + jnp.arange(order_count)).astype(jnp.float32)
    legendre = legendre_table(orders, mode_count, jnp.cos(colat_grid), jnp.sin(colat_grid))
    quadrature = 2.0 * jnp.pi * jnp.pi * jnp.sin(colat_grid) / lat_count
    weighted = legendre * quadrature
    coeffs = jnp.einsum("inc,nrk->irkc", first_sliced, forward, precision=highest)
    spectrum = jnp.einsum(
        "kli,irkc->lrkc",
        weighted,
        lax.all_to_all(coeffs, "lat", split_axis=2, concat_axis=0, tiled=True),
        precision=highest,
    )
    spectrum = spectrum * filter_gains[:, None, None, :]
    restored = jnp.einsum("kli,lrkc->irkc", legendre, spectrum, precision=highest)
    returned = lax.all_to_all(restored, "lat", split_axis=0, concat_axis=2, tiled=True)
    filtered = jnp.einsum("irkc,rkn->inc", returned, inverse, precision=highest)
    second_taps = lax.dynamic_slice_in_dim(conv_second, channel_start, slice_width, 1)
    second_sliced = first_sliced + filtered
    incoming = second_sliced + slice_stencil(second_sliced, second_taps)
    arrived = lax.all_to_all(incoming, "lon", split_axis=1, concat_axis=2, tiled=True)
    return channel_mlp(arrived, norm_gain, up_weight, down_weight)


LANES = 128
TILE = 8
bf16 = jnp.bfloat16
f32 = jnp.float32


def legendre_numpy(modes, lat_count):
    theta = np.pi * (np.arange(lat_count) + 0.5) / lat_count
    cosine, sine = np.cos(theta), np.sin(theta)
    table = np.zeros((modes, modes, lat_count))
    for m in range(modes):
        seed = 0.5 * (
            math.log((2 * m + 1) / (4 * math.pi))
            + math.lgamma(2 * m + 1)
            - 2 * m * math.log(2.0)
            - 2 * math.lgamma(m + 1)
        )
        table[m, m] = np.exp(seed + m * np.log(sine))
        for l in range(m + 1, modes):
            a = math.sqrt((4.0 * l * l - 1) / (l * l - m * m))
            b = math.sqrt(max((l - 1.0) ** 2 - m * m, 0.0) / (4.0 * (l - 1.0) ** 2 - 1)) if l > 1 else 0.0
            earlier = table[m, l - 2] if l > m + 1 else 0.0
            table[m, l] = a * (cosine * table[m, l - 1] - b * earlier)
    quadrature = 2 * np.pi**2 * sine / lat_count
    return table, table * quadrature


def split_numpy(table):
    high = table.astype(np.float32).astype(jnp.bfloat16)
    low = (table - high.astype(np.float64)).astype(np.float32).astype(jnp.bfloat16)
    return np.stack([high, low])


@functools.lru_cache(maxsize=None)
def constant_tables(nl, nj, rows, cols, modes):
    lat_count, lon_count = rows * nl, cols * nj
    rs = rows // nj
    pair = TILE // rs // 2
    groups = modes // nl // pair
    n = np.arange(lon_count)
    k = np.arange(modes)
    phase = 2 * np.pi * ((k[:, None] * n[None, :]) % lon_count) / lon_count
    trig = np.stack([np.cos(phase), -np.sin(phase)], axis=1)
    factor = np.where(k == 0, 1.0, 2.0)
    same = np.eye(rs)
    by_order = trig.reshape(nl, groups, pair, 2, lon_count)
    forward = by_order.reshape(nl, groups, pair, 2, nj, cols) / lon_count
    forward = np.einsum("lqopjn,rs->lqropjsn", forward, same)
    forward = forward.reshape(modes * 2 * rs, nj * rs * cols)
    wide = cols + 4
    where = (np.arange(nj)[:, None] * cols + np.arange(wide)[None, :] - 2) % lon_count
    back = (trig * factor[:, None, None]).reshape(nl, groups, pair, 2, lon_count)[..., where]
    back = np.einsum("lqopjn,rs->jrnlqsop", back, same)
    back = back.reshape(nj * rs * wide, modes * 2 * rs)
    pick = np.zeros((nj, wide, lon_count))
    pick[np.arange(nj)[:, None], np.arange(wide)[None, :], where] = 1.0
    pick = np.einsum("jwtn,rs->jrwtsn", pick.reshape(nj, wide, nj, cols), same)
    pick = pick.reshape(nj * rs * wide, nj * rs * cols)
    table, weighted = legendre_numpy(modes, lat_count)

    def by_lat(values):
        room = -values.shape[2] % (LANES // 2)
        parts = split_numpy(np.pad(values, ((0, 0), (0, 0), (0, room))))
        parts = np.concatenate([parts[0], parts[1]], axis=-1)
        return parts.reshape((nl, modes // nl) + parts.shape[1:])

    return (
        split_numpy(forward),
        split_numpy(back),
        pick.astype(jnp.bfloat16),
        by_lat(weighted),
        by_lat(np.swapaxes(table, 1, 2)),
    )


def halves(value):
    high = value.astype(bf16)
    return high, (value - high.astype(f32)).astype(bf16)


def mm(a, b):
    return jnp.dot(a, b, preferred_element_type=f32)


def mm3(a_high, a_low, b):
    high, low = halves(b)
    return mm(a_high, high) + (mm(a_high, low) + mm(a_low, high))


def mm_packed(table, value):
    depth = table.shape[1] // 2
    if value.shape[0] < depth:
        blank = jnp.zeros((depth - value.shape[0], value.shape[1]), f32)
        value = jnp.concatenate([value, blank], axis=0)
    high, low = halves(value)
    return mm(
        jnp.concatenate([table, table[:, :depth]], axis=1),
        jnp.concatenate([high, high, low], axis=0),
    )


def stencil_block(source, taps, cols, rows, width):
    totals = [None] * rows
    for r in range(rows + 4):
        base = source[r, :, cols]
        for b in range(5):
            moved = base if b == 0 else pltpu.roll(base, base.shape[0] - b, 0)
            for a in range(5):
                i = r - a
                if 0 <= i < rows:
                    term = taps[a * 5 + b : a * 5 + b + 1, cols] * moved
                    if a == 2 and b == 2:
                        term = term + moved
                    totals[i] = term if totals[i] is None else totals[i] + term
    return [total[:width] for total in totals]


def block_kernel(
    nl, nj, rows,
    latent, taps1, taps2, gains, norm_gain, fwd, back, pick, up_hbm, down_hbm, wt_hbm, pt_hbm,
    out,
    grid, row_out, row_in, west_out, east_out, west_in, east_in, first_pad, mine, circle, sent_c, spec_in,
    spec_out, got_c, wide_out, second_pad, gain_in, gain_all, third, up, down, wt, pt,
    load_sem, in_sem, out_sem, row_s, row_r, col_s, col_r, gain_s, gain_r, a_s, a_r, c_s, c_r, b_s, b_r, z_s, z_r,
    halo_s, halo_r,
):
    channels = latent.shape[1]
    cols = latent.shape[0] // rows
    wide = cols + 4
    blocks = channels // LANES
    rs = rows // nj
    part = rs * cols
    total = nl * nj
    per = spec_in.shape[0]
    orders = wt.shape[0]
    pair = TILE // rs // 2
    groups = orders // pair
    units = groups * blocks
    lat_count = rows * nl
    la, lo = lax.axis_index("lat"), lax.axis_index("lon")
    me = la * nj + lo
    above, below = lax.rem(la + nl - 1, nl), lax.rem(la + 1, nl)
    right, left = lax.rem(lo + 1, nj), lax.rem(lo + nj - 1, nj)
    has_above, has_below = la > 0, la < nl - 1

    def span(start, size):
        return pl.ds(start if isinstance(start, int) else pl.multiple_of(start, TILE), size)

    def lanes(block):
        return pl.ds(block * LANES, LANES)

    def rcopy(src, dst, send, recv, a, b):
        return pltpu.make_async_remote_copy(
            src_ref=src, dst_ref=dst, send_sem=send, recv_sem=recv,
            device_id={"lat": a, "lon": b}, device_id_type=pl.DeviceIdType.MESH,
        )

    loads = [
        pltpu.make_async_copy(wt_hbm.at[la], wt, load_sem.at[0]),
        pltpu.make_async_copy(pt_hbm.at[la], pt, load_sem.at[1]),
        pltpu.make_async_copy(up_hbm, up, load_sem.at[2]),
        pltpu.make_async_copy(down_hbm, down, load_sem.at[3]),
    ]

    def in_copy(block):
        return pltpu.make_async_copy(latent.at[:, lanes(block)], grid.at[block], in_sem.at[block])

    def out_copy(block):
        return pltpu.make_async_copy(grid.at[block], out.at[:, lanes(block)], out_sem.at[block])

    for block in range(blocks):
        in_copy(block).start()
    for load in loads:
        load.start()

    barrier = pltpu.get_barrier_semaphore()

    def greet(d, carry):
        peer = lax.rem(me + d, total)
        pl.semaphore_signal(
            barrier, inc=1, device_id={"lat": peer // nj, "lon": lax.rem(peer, nj)},
            device_id_type=pl.DeviceIdType.MESH,
        )
        return carry

    lax.fori_loop(1, total, greet, 0)
    for block in range(blocks):
        in_copy(block).wait()
        for i in range(rows):
            line = grid[block, pl.ds(i, cols, stride=rows), :]
            first_pad[2 + i, 2 : cols + 2, lanes(block)] = line
            west_out[i, :, lanes(block)] = line[:2]
            east_out[i, :, lanes(block)] = line[cols - 2 :]
            if i < 2:
                row_out[1, i, :, lanes(block)] = line
            if i >= rows - 2:
                row_out[0, i - rows + 2, :, lanes(block)] = line
    blank = jnp.zeros((2, wide, channels), f32)
    for absent, place in ((la == 0, pl.ds(0, 2)), (la == nl - 1, pl.ds(rows + 2, 2))):
        @pl.when(absent)
        def _(place=place):
            first_pad[place] = blank
            second_pad[place] = blank
    pl.semaphore_wait(barrier, total - 1)

    halos = [
        (has_below, has_above,
         rcopy(row_out.at[0], row_in.at[0], row_s.at[0], row_r.at[0], below, lo)),
        (has_above, has_below,
         rcopy(row_out.at[1], row_in.at[1], row_s.at[1], row_r.at[1], above, lo)),
    ]
    for side, (source, target, to) in enumerate(((east_out, west_in, right), (west_out, east_in, left))):
        s, r = col_s.at[side], col_r.at[side]
        halos += [
            (None, None, rcopy(source, target.at[pl.ds(2, rows)], s.at[0], r.at[0], la, to)),
            (has_below, has_above,
             rcopy(source.at[pl.ds(rows - 2, 2)], target.at[pl.ds(0, 2)], s.at[1], r.at[1], below, to)),
            (has_above, has_below,
             rcopy(source.at[pl.ds(0, 2)], target.at[pl.ds(rows + 2, 2)], s.at[2], r.at[2], above, to)),
        ]

    def guarded(guard, action):
        if guard is None:
            action()
        else:
            pl.when(guard)(action)

    for send, _, copy in halos:
        guarded(send, copy.start)
    gain_copies = []
    for d in range(1, nj):
        gain_copies.append(
            rcopy(gains, gain_in.at[lo], gain_s.at[d], gain_r.at[d], la, lax.rem(lo + d, nj))
        )
    for copy in gain_copies:
        copy.start()
    gain_in[lo] = gains[...]
    for _, arrive, copy in halos:
        guarded(arrive, copy.wait_recv)
    for side, (guard, base) in enumerate(((has_above, 0), (has_below, rows + 2))):
        @pl.when(guard)
        def _(side=side, base=base):
            for i in range(2):
                first_pad[base + i, 2 : cols + 2, :] = row_in[side, i]
                first_pad[base + i, 0:2, :] = west_in[base + i]
                first_pad[base + i, cols + 2 : wide, :] = east_in[base + i]
    for i in range(rows):
        first_pad[2 + i, 0:2, :] = west_in[2 + i]
        first_pad[2 + i, cols + 2 : wide, :] = east_in[2 + i]

    def a_copy(block, d):
        to = lax.rem(lo + d, nj)
        return rcopy(
            mine.at[span(to * part, part), lanes(block)], circle.at[lo, :, lanes(block)],
            a_s.at[block, d], a_r.at[block, d], la, to,
        )

    def z_copy(block, d):
        to = lax.rem(lo + d, nj)
        return rcopy(
            wide_out.at[pl.ds(to * rs, rs), :, lanes(block)],
            second_pad.at[pl.ds(2 + lo * rs, rs), :, lanes(block)],
            z_s.at[block, d], z_r.at[block, d], la, to,
        )

    def c_copy(t, a, b, source):
        return rcopy(
            sent_c.at[a, nj * t + b], spec_in.at[t, span(source * TILE, TILE), :],
            c_s.at[t], c_r.at[t], a, b,
        )

    def b_copy(t, a, b, la, lo):
        peer = a * nj + b
        return rcopy(
            spec_out.at[t, span(peer * TILE, TILE), :], got_c.at[la, nj * t + lo],
            b_s.at[t], b_r.at[t], a, b,
        )

    def keep_c(t):
        spec_in[t, span(me * TILE, TILE), :] = sent_c[la, nj * t + lo]

    def others(action):
        def step(d, carry):
            peer = lax.rem(me + d, total)
            action(peer, lax.div(peer, nj), lax.rem(peer, nj))
            return carry

        lax.fori_loop(1, total, step, 0)

    def tiles(t, count, send, recv):
        block = spec_in.at[t, pl.ds(0, count * TILE), :]
        return rcopy(block, block, send.at[t], recv.at[t], below, right)

    def partners(t, action):
        owners = min(nj, units - nj * t)
        if owners == nj:
            action(total - 1)
        else:
            pl.when(lo < owners)(lambda: action(nl * owners - 1))
            pl.when(lo >= owners)(lambda: action(nl * owners))

    def own_unit(t, action):
        if nj * t + nj <= units:
            action()
        else:
            pl.when(nj * t + lo < units)(action)

    def real_unit(t, b, action):
        if nj * t + nj <= units:
            action()
        else:
            pl.when(nj * t + b < units)(action)

    for block in range(blocks):
        sums = stencil_block(first_pad, taps1, lanes(block), rows, cols)
        for i in range(rows):
            mine[cols * i : cols * (i + 1), lanes(block)] = sums[i][:cols]
        for d in range(1, nj):
            a_copy(block, d).start()
        circle[lo, :, lanes(block)] = mine[span(lo * part, part), lanes(block)]

    for block in range(blocks):
        for d in range(1, nj):
            a_copy(block, d).wait_recv()
        values = circle[:, :, lanes(block)].reshape(nj * part, LANES)
        coeffs = mm3(fwd[0], fwd[1], values)
        sent_c[:, block * groups : (block + 1) * groups] = coeffs.reshape(nl, groups, TILE, LANES)
        for t in range(per):
            if (min(nj * (t + 1), units) - 1) // groups == block:
                others(lambda peer, a, b, t=t: real_unit(t, b, c_copy(t, a, b, me).start))
                own_unit(t, lambda t=t: keep_c(t))

    for copy in gain_copies:
        copy.wait_recv()
    width = gains.shape[1]
    for j in range(nj):
        gain_all[:, width * j : width * (j + 1)] = gain_in[j]
    loads[0].wait()
    loads[1].wait()

    def filter_unit(t):
        tiles(t, total - 1, c_s, c_r).wait_recv()
        unit = nj * t + lo
        block = unit // groups
        group = lax.rem(unit, groups)
        gain = gain_all[:, pl.ds(pl.multiple_of(block * LANES, LANES), LANES)]
        gain = jnp.concatenate([gain, gain], axis=1)
        for o in range(pair):
            data = jnp.concatenate(
                [spec_in[t, pl.ds(2 * o + ri, lat_count, stride=2 * pair), :] for ri in range(2)], axis=1
            )
            order = group * pair + o
            restored = mm_packed(pt[order], mm_packed(wt[order], data) * gain)
            for ri in range(2):
                spec_out[t, pl.ds(2 * o + ri, lat_count, stride=2 * pair), :] = (
                    restored[:, ri * LANES : (ri + 1) * LANES]
                )
        others(lambda peer, a, b: b_copy(t, a, b, la, lo).start())
        got_c[la, nj * t + lo] = spec_out[t, span(me * TILE, TILE), :]

    for t in range(per):
        own_unit(t, lambda t=t: filter_unit(t))

    taken = set()
    for block in range(blocks):
        for unit in range(block * groups, (block + 1) * groups):
            t = unit // nj
            if t not in taken:
                taken.add(t)
                partners(t, lambda count, t=t: tiles(t, count, b_s, b_r).wait_recv())
        coeffs = got_c[:, block * groups : (block + 1) * groups].reshape(nl * groups * TILE, LANES)
        values = circle[:, :, lanes(block)].reshape(nj * part, LANES)
        high, low = halves(values)
        rebuilt = mm3(back[0], back[1], coeffs) + (mm(pick[...], low) + mm(pick[...], high))
        wide_out[:, :, lanes(block)] = rebuilt.reshape(nj * rs, wide, LANES)
        for d in range(1, nj):
            z_copy(block, d).start()
        second_pad[pl.ds(2 + lo * rs, rs), :, lanes(block)] = wide_out[pl.ds(lo * rs, rs), :, lanes(block)]

    def row_copies(block):
        edge = second_pad.at[:, :, lanes(block)]
        return (
            (has_below, has_above,
             rcopy(edge.at[pl.ds(rows, 2)], edge.at[pl.ds(0, 2)], halo_s.at[block, 0], halo_r.at[block, 0], below, lo)),
            (has_above, has_below,
             rcopy(edge.at[pl.ds(2, 2)], edge.at[pl.ds(rows + 2, 2)], halo_s.at[block, 1], halo_r.at[block, 1], above, lo)),
        )

    for block in range(blocks):
        for d in range(1, nj):
            z_copy(block, d).wait_recv()
        for send, _, copy in row_copies(block):
            guarded(send, copy.start)
    for block in range(blocks):
        for _, arrive, copy in row_copies(block):
            guarded(arrive, copy.wait_recv)
        sums = stencil_block(second_pad, taps2, lanes(block), rows, cols)
        for i in range(rows):
            third[cols * i : cols * (i + 1), lanes(block)] = sums[i][:cols]

    loads[2].wait()
    loads[3].wait()
    state = third[...]
    average = jnp.mean(state, axis=-1, keepdims=True)
    centred = state - average
    spread = jnp.mean(centred * centred, axis=-1, keepdims=True)
    normed = (centred * lax.rsqrt(spread + 1e-05) * norm_gain[...].reshape(1, channels)).astype(bf16)
    active = jax.nn.gelu(mm(normed, up[...]), approximate=True).astype(bf16)
    third[...] = state + mm(active, down[...])
    for block in range(blocks):
        for i in range(rows):
            grid[block, pl.ds(i, cols, stride=rows), :] = third[cols * i : cols * (i + 1), lanes(block)]
        out_copy(block).start()

    for block in range(blocks):
        out_copy(block).wait()
    for send, _, copy in halos:
        guarded(send, copy.wait_send)
    for copy in gain_copies:
        copy.wait_send()
    for block in range(blocks):
        for d in range(1, nj):
            a_copy(block, d).wait_send()
            z_copy(block, d).wait_send()
        for send, _, copy in row_copies(block):
            guarded(send, copy.wait_send)

    for t in range(per):
        partners(t, lambda count, t=t: tiles(t, count, c_s, c_r).wait_send())
        own_unit(t, lambda t=t: tiles(t, total - 1, b_s, b_r).wait_send())


def fused(nl, nj, latent, conv_first, conv_second, filter_gains, norm_gain, up_weight, down_weight):
    rows, cols, channels = latent.shape
    modes, width = filter_gains.shape
    forward, back, pick, wt, pt = (jnp.asarray(t) for t in constant_tables(nl, nj, rows, cols, modes))
    rs = rows // nj
    wide = cols + 4
    blocks = channels // LANES
    total = nl * nj
    groups = modes // nl // (TILE // rs // 2)
    per = -(-groups * blocks // nj)
    vm = lambda *shape, kind=f32: pltpu.VMEM(shape, kind)
    dma = lambda *shape: pltpu.SemaphoreType.DMA(shape)
    here = pl.BlockSpec(memory_space=pltpu.VMEM)
    far = pl.BlockSpec(memory_space=pltpu.HBM)
    result = pl.pallas_call(
        functools.partial(block_kernel, nl, nj, rows),
        out_shape=jax.ShapeDtypeStruct((cols * rows, channels), f32),
        in_specs=[far] + [here] * 7 + [far] * 4,
        out_specs=far,
        scratch_shapes=[
            vm(blocks, cols * rows, LANES),
            vm(2, 2, cols, channels),
            vm(2, 2, cols, channels),
            vm(rows, 2, channels),
            vm(rows, 2, channels),
            vm(rows + 4, 2, channels),
            vm(rows + 4, 2, channels),
            vm(rows + 4, wide, channels),
            vm(rows * cols, channels),
            vm(nj, rs * cols, channels),
            vm(nl, per * nj, TILE, LANES),
            vm(per, total * TILE, LANES),
            vm(per, total * TILE, LANES),
            vm(nl, per * nj, TILE, LANES),
            vm(nj * rs, wide, channels),
            vm(rows + 4, wide, channels),
            vm(nj, modes, width),
            vm(modes, channels),
            vm(rows * cols, channels),
            vm(*up_weight.shape, kind=bf16),
            vm(*down_weight.shape, kind=bf16),
            vm(*wt.shape[1:], kind=bf16),
            vm(*pt.shape[1:], kind=bf16),
            dma(4), dma(blocks), dma(blocks),
            dma(2), dma(2), dma(2, 3), dma(2, 3), dma(nj), dma(nj),
            dma(blocks, nj), dma(blocks, nj), dma(per), dma(per), dma(per), dma(per),
            dma(blocks, nj), dma(blocks, nj), dma(blocks, 2), dma(blocks, 2),
        ],
        compiler_params=pltpu.CompilerParams(
            collective_id=0, has_side_effects=True, vmem_limit_bytes=60 * 1024 * 1024
        ),
        name="block",
    )(
        jnp.swapaxes(latent, 0, 1).reshape(cols * rows, channels), conv_first, conv_second,
        filter_gains, norm_gain, forward, back, pick, up_weight, down_weight, wt, pt,
    )
    return jnp.swapaxes(result.reshape(cols, rows, channels), 0, 1)


def fits(nl, nj, latent, filter_gains):
    rows, cols, channels = latent.shape
    modes = filter_gains.shape[0]
    if rows % nj or channels % LANES or modes % nl or nj < 2 or nl < 2:
        return False
    rs = rows // nj
    if TILE % (2 * rs) or (rs * cols) % TILE or (cols + 4) % TILE:
        return False
    if modes > LANES // 2 or rows * nl > LANES // 2:
        return False
    return (modes // nl) % (TILE // rs // 2) == 0


def body(latent, conv_first, conv_second, filter_gains, norm_gain, up_weight, down_weight):
    nl, nj = lax.axis_size("lat"), lax.axis_size("lon")
    arguments = (latent, conv_first, conv_second, filter_gains, norm_gain, up_weight, down_weight)
    if fits(nl, nj, latent, filter_gains):
        return fused(nl, nj, *arguments)
    return per_device(*arguments)


def solution(mesh):
    return jax.shard_map(
        body,
        mesh=mesh,
        in_specs=(P("lat", "lon", None), P(), P(), P(None, "lon"), P(), P(), P()),
        out_specs=P("lat", "lon", None),
        check_vma=False,
    )
```

```python
import functools
import math

import jax
import jax.numpy as jnp
import numpy as np
from jax import lax
from jax.experimental import pallas as pl
from jax.experimental.pallas import tpu as pltpu
from jax.sharding import PartitionSpec as P

highest = lax.Precision.HIGHEST


def padded_2(block, sides, width):
    for axis, dim in sides:
        count = lax.axis_size(axis)
        forward = [(i, i + 1) for i in range(count - 1)]
        backward = [(target, source) for source, target in forward]
        low = lax.ppermute(
            lax.slice_in_dim(block, block.shape[dim] - width, None, axis=dim), axis, forward
        )
        high = lax.ppermute(lax.slice_in_dim(block, 0, width, axis=dim), axis, backward)
        block = jnp.concatenate([low, block, high], axis=dim)
    return block


def stencil_sum(padded, weights, row_count, col_count):
    stencil_total = jnp.zeros((row_count, col_count, padded.shape[2]), padded.dtype)
    for row_shift in range(5):
        for col_shift in range(5):
            stencil_total = (
                stencil_total
                + weights[row_shift * 5 + col_shift]
                * padded[row_shift : row_shift + row_count, col_shift : col_shift + col_count, :]
            )
    return stencil_total


def slice_stencil(sliced, weights):
    lat_extended = padded_2(sliced, (("lat", 0),), 2)
    wrapped = jnp.concatenate([lat_extended[:, -2:], lat_extended, lat_extended[:, :2]], axis=1)
    return stencil_sum(wrapped, weights, sliced.shape[0], sliced.shape[1])


def colatitude(cell_count, float_type):
    cell_index = jnp.arange(cell_count).astype(float_type)
    return jnp.pi * (cell_index + 0.5) / cell_count


def legendre_table(orders, degrees, cosine, sine_theta):
    log_seed = 0.5 * (
        jnp.log((2.0 * orders + 1.0) / (4.0 * jnp.pi))
        + jax.scipy.special.gammaln(2.0 * orders + 1.0)
        - 2.0 * orders * jnp.log(2.0)
        - 2.0 * jax.scipy.special.gammaln(orders + 1.0)
    )
    diagonal_term = jnp.exp(log_seed[:, None] + orders[:, None] * jnp.log(sine_theta)[None, :])
    blanks = jnp.zeros_like(diagonal_term)
    legendre = jnp.zeros((orders.shape[0], degrees, sine_theta.shape[0]), diagonal_term.dtype)

    def block_step(block_index, state_tuple):
        previous, earlier, legendre = state_tuple
        values = []
        for offset in range(8):
            degree = (block_index * 8 + offset).astype(diagonal_term.dtype)
            square = degree * degree
            upper_ratio = jnp.sqrt(
                jnp.maximum(4.0 * square - 1.0, 1.0) / jnp.maximum(square - orders * orders, 1.0)
            )
            below_sq = (degree - 1.0) * (degree - 1.0)
            lower_ratio = jnp.sqrt(
                jnp.maximum(below_sq - orders * orders, 0.0)
                / jnp.maximum(4.0 * below_sq - 1.0, 1.0)
            )
            recurred = upper_ratio[:, None] * (
                cosine[None, :] * previous - lower_ratio[:, None] * earlier
            )
            current = jnp.where(
                (degree < orders)[:, None],
                blanks,
                jnp.where((degree == orders)[:, None], diagonal_term, recurred),
            )
            values.append(current)
            earlier = previous
            previous = current
        stacked = jnp.stack(values, axis=1)
        legendre = lax.dynamic_update_slice(
            legendre, stacked, (jnp.int32(0), (block_index * 8).astype(jnp.int32), jnp.int32(0))
        )
        return (previous, earlier, legendre)

    return lax.fori_loop(0, degrees // 8, block_step, (blanks, blanks, legendre))[2]


def fourier_tables(lon_count, mode_count, float_type):
    product_index = jnp.arange(lon_count)[:, None] * jnp.arange(mode_count)[None, :] % lon_count
    phase_grid = 2.0 * jnp.pi * product_index.astype(float_type) / lon_count
    forward = jnp.stack([jnp.cos(phase_grid), -jnp.sin(phase_grid)], axis=1) / lon_count
    factor = jnp.where(jnp.arange(mode_count) == 0, 1.0, 2.0).astype(float_type)
    inverse = jnp.stack(
        [jnp.cos(phase_grid).T * factor[:, None], -jnp.sin(phase_grid).T * factor[:, None]], axis=0
    )
    return (forward, inverse)


def channel_mlp(latent, norm_gain, up_weight, down_weight):
    average = jnp.mean(latent, axis=-1, keepdims=True)
    centred = latent - average
    spread = jnp.mean(centred * centred, axis=-1, keepdims=True)
    normed = (centred * lax.rsqrt(spread + 1e-05) * norm_gain).astype(jnp.bfloat16)
    hidden = jnp.dot(normed, up_weight, preferred_element_type=jnp.float32)
    active = jax.nn.gelu(hidden, approximate=True).astype(jnp.bfloat16)
    return latent + jnp.dot(active, down_weight, preferred_element_type=jnp.float32)


def per_device(latent, conv_first, conv_second, filter_gains, norm_gain, up_weight, down_weight):
    lat_size = lax.axis_size("lat")
    lon_size = lax.axis_size("lon")
    lat_local = latent.shape[0]
    lon_local = latent.shape[1]
    slice_width = filter_gains.shape[1]
    mode_count = filter_gains.shape[0]
    lat_count = lat_local * lat_size
    lon_count = lon_local * lon_size
    order_count = mode_count // lat_size
    channel_start = lax.axis_index("lon") * slice_width
    sliced = lax.all_to_all(latent, "lon", split_axis=2, concat_axis=1, tiled=True)
    first_taps = lax.dynamic_slice_in_dim(conv_first, channel_start, slice_width, 1)
    first_sliced = sliced + slice_stencil(sliced, first_taps)
    forward, inverse = fourier_tables(lon_count, mode_count, jnp.float32)
    colat_grid = colatitude(lat_count, jnp.float32)
    orders = (lax.axis_index("lat") * order_count + jnp.arange(order_count)).astype(jnp.float32)
    legendre = legendre_table(orders, mode_count, jnp.cos(colat_grid), jnp.sin(colat_grid))
    quadrature = 2.0 * jnp.pi * jnp.pi * jnp.sin(colat_grid) / lat_count
    weighted = legendre * quadrature
    coeffs = jnp.einsum("inc,nrk->irkc", first_sliced, forward, precision=highest)
    spectrum = jnp.einsum(
        "kli,irkc->lrkc",
        weighted,
        lax.all_to_all(coeffs, "lat", split_axis=2, concat_axis=0, tiled=True),
        precision=highest,
    )
    spectrum = spectrum * filter_gains[:, None, None, :]
    restored = jnp.einsum("kli,lrkc->irkc", legendre, spectrum, precision=highest)
    returned = lax.all_to_all(restored, "lat", split_axis=0, concat_axis=2, tiled=True)
    filtered = jnp.einsum("irkc,rkn->inc", returned, inverse, precision=highest)
    second_taps = lax.dynamic_slice_in_dim(conv_second, channel_start, slice_width, 1)
    second_sliced = first_sliced + filtered
    incoming = second_sliced + slice_stencil(second_sliced, second_taps)
    arrived = lax.all_to_all(incoming, "lon", split_axis=1, concat_axis=2, tiled=True)
    return channel_mlp(arrived, norm_gain, up_weight, down_weight)


LANES = 128
TILE = 8
bf16 = jnp.bfloat16
f32 = jnp.float32


def legendre_numpy(modes, lat_count):
    theta = np.pi * (np.arange(lat_count) + 0.5) / lat_count
    cosine, sine = np.cos(theta), np.sin(theta)
    table = np.zeros((modes, modes, lat_count))
    for m in range(modes):
        seed = 0.5 * (
            math.log((2 * m + 1) / (4 * math.pi))
            + math.lgamma(2 * m + 1)
            - 2 * m * math.log(2.0)
            - 2 * math.lgamma(m + 1)
        )
        table[m, m] = np.exp(seed + m * np.log(sine))
        for l in range(m + 1, modes):
            a = math.sqrt((4.0 * l * l - 1) / (l * l - m * m))
            b = math.sqrt(max((l - 1.0) ** 2 - m * m, 0.0) / (4.0 * (l - 1.0) ** 2 - 1)) if l > 1 else 0.0
            earlier = table[m, l - 2] if l > m + 1 else 0.0
            table[m, l] = a * (cosine * table[m, l - 1] - b * earlier)
    quadrature = 2 * np.pi**2 * sine / lat_count
    return table, table * quadrature


def split_numpy(table):
    high = table.astype(np.float32).astype(jnp.bfloat16)
    low = (table - high.astype(np.float64)).astype(np.float32).astype(jnp.bfloat16)
    return np.stack([high, low])


@functools.lru_cache(maxsize=None)
def constant_tables(nl, nj, rows, cols, modes):
    lat_count, lon_count = rows * nl, cols * nj
    rs = rows // nj
    pair = TILE // rs // 2
    groups = modes // nl // pair
    n = np.arange(lon_count)
    k = np.arange(modes)
    phase = 2 * np.pi * ((k[:, None] * n[None, :]) % lon_count) / lon_count
    trig = np.stack([np.cos(phase), -np.sin(phase)], axis=1)
    factor = np.where(k == 0, 1.0, 2.0)
    same = np.eye(rs)
    by_order = trig.reshape(nl, groups, pair, 2, lon_count)
    forward = by_order.reshape(nl, groups, pair, 2, nj, cols) / lon_count
    forward = np.einsum("lqopjn,rs->lqropjsn", forward, same)
    forward = forward.reshape(modes * 2 * rs, nj * rs * cols)
    wide = cols + 4
    where = (np.arange(nj)[:, None] * cols + np.arange(wide)[None, :] - 2) % lon_count
    back = (trig * factor[:, None, None]).reshape(nl, groups, pair, 2, lon_count)[..., where]
    back = np.einsum("lqopjn,rs->jrnlqsop", back, same)
    back = back.reshape(nj * rs * wide, modes * 2 * rs)
    pick = np.zeros((nj, wide, lon_count))
    pick[np.arange(nj)[:, None], np.arange(wide)[None, :], where] = 1.0
    pick = np.einsum("jwtn,rs->jrwtsn", pick.reshape(nj, wide, nj, cols), same)
    pick = pick.reshape(nj * rs * wide, nj * rs * cols)
    table, weighted = legendre_numpy(modes, lat_count)

    def by_lat(values):
        room = -values.shape[2] % (LANES // 2)
        parts = split_numpy(np.pad(values, ((0, 0), (0, 0), (0, room))))
        parts = np.concatenate([parts[0], parts[1]], axis=-1)
        return parts.reshape((nl, modes // nl) + parts.shape[1:])

    return (
        split_numpy(forward),
        split_numpy(back),
        pick.astype(jnp.bfloat16),
        by_lat(weighted),
        by_lat(np.swapaxes(table, 1, 2)),
    )


def halves(value):
    high = value.astype(bf16)
    return high, (value - high.astype(f32)).astype(bf16)


def mm(a, b):
    return jnp.dot(a, b, preferred_element_type=f32)


def mm3(a_high, a_low, b):
    high, low = halves(b)
    return mm(a_high, high) + (mm(a_high, low) + mm(a_low, high))


def mm_packed(table, value):
    depth = table.shape[1] // 2
    if value.shape[0] < depth:
        blank = jnp.zeros((depth - value.shape[0], value.shape[1]), f32)
        value = jnp.concatenate([value, blank], axis=0)
    high, low = halves(value)
    return mm(
        jnp.concatenate([table, table[:, :depth]], axis=1),
        jnp.concatenate([high, high, low], axis=0),
    )


def stencil_block(source, taps, cols, rows, width):
    totals = [None] * rows
    for r in range(rows + 4):
        base = source[r, :, cols]
        for b in range(5):
            moved = base if b == 0 else pltpu.roll(base, base.shape[0] - b, 0)
            for a in range(5):
                i = r - a
                if 0 <= i < rows:
                    term = taps[a * 5 + b : a * 5 + b + 1, cols] * moved
                    if a == 2 and b == 2:
                        term = term + moved
                    totals[i] = term if totals[i] is None else totals[i] + term
    return [total[:width] for total in totals]


def block_kernel(
    nl, nj, rows,
    latent, taps1, taps2, gains, norm_gain, fwd, back, pick, up_hbm, down_hbm, wt_hbm, pt_hbm,
    out,
    grid, row_out, row_in, west_out, east_out, west_in, east_in, first_pad, mine, circle, sent_c, spec_in,
    spec_out, got_c, wide_out, second_pad, gain_in, gain_all, third, up, down, wt, pt,
    load_sem, in_sem, out_sem, row_s, row_r, col_s, col_r, gain_s, gain_r, a_s, a_r, c_s, c_r, b_s, b_r, z_s, z_r,
    halo_s, halo_r,
):
    channels = latent.shape[1]
    cols = latent.shape[0] // rows
    wide = cols + 4
    blocks = channels // LANES
    rs = rows // nj
    part = rs * cols
    total = nl * nj
    per = spec_in.shape[0]
    orders = wt.shape[0]
    pair = TILE // rs // 2
    groups = orders // pair
    units = groups * blocks
    lat_count = rows * nl
    la, lo = lax.axis_index("lat"), lax.axis_index("lon")
    me = la * nj + lo
    above, below = lax.rem(la + nl - 1, nl), lax.rem(la + 1, nl)
    right, left = lax.rem(lo + 1, nj), lax.rem(lo + nj - 1, nj)
    has_above, has_below = la > 0, la < nl - 1

    def span(start, size):
        return pl.ds(start if isinstance(start, int) else pl.multiple_of(start, TILE), size)

    def lanes(block):
        return pl.ds(block * LANES, LANES)

    def rcopy(src, dst, send, recv, a, b):
        return pltpu.make_async_remote_copy(
            src_ref=src, dst_ref=dst, send_sem=send, recv_sem=recv,
            device_id={"lat": a, "lon": b}, device_id_type=pl.DeviceIdType.MESH,
        )

    loads = [
        pltpu.make_async_copy(wt_hbm.at[la], wt, load_sem.at[0]),
        pltpu.make_async_copy(pt_hbm.at[la], pt, load_sem.at[1]),
        pltpu.make_async_copy(up_hbm, up, load_sem.at[2]),
        pltpu.make_async_copy(down_hbm, down, load_sem.at[3]),
    ]

    def in_copy(block):
        return pltpu.make_async_copy(latent.at[:, lanes(block)], grid.at[block], in_sem.at[block])

    def out_copy(block):
        return pltpu.make_async_copy(grid.at[block], out.at[:, lanes(block)], out_sem.at[block])

    for block in range(blocks):
        in_copy(block).start()
    for load in loads:
        load.start()

    barrier = pltpu.get_barrier_semaphore()

    def greet(a, b):
        pl.semaphore_signal(
            barrier, inc=1, device_id={"lat": a, "lon": b}, device_id_type=pl.DeviceIdType.MESH
        )

    def greet_band(d, carry):
        a = lax.rem(la + d, nl)
        for b in range(nj):
            greet(a, b)
        return carry

    for d in range(1, nj):
        greet(la, lax.rem(lo + d, nj))
    lax.fori_loop(1, nl, greet_band, 0)
    for block in range(blocks):
        in_copy(block).wait()
        for i in range(rows):
            line = grid[block, pl.ds(i, cols, stride=rows), :]
            first_pad[2 + i, 2 : cols + 2, lanes(block)] = line
            west_out[i, :, lanes(block)] = line[:2]
            east_out[i, :, lanes(block)] = line[cols - 2 :]
            if i < 2:
                row_out[1, i, :, lanes(block)] = line
            if i >= rows - 2:
                row_out[0, i - rows + 2, :, lanes(block)] = line
    blank = jnp.zeros((2, wide, channels), f32)
    for absent, place in ((la == 0, pl.ds(0, 2)), (la == nl - 1, pl.ds(rows + 2, 2))):
        @pl.when(absent)
        def _(place=place):
            first_pad[place] = blank
            second_pad[place] = blank
    pl.semaphore_wait(barrier, total - 1)

    halos = [
        (has_below, has_above,
         rcopy(row_out.at[0], row_in.at[0], row_s.at[0], row_r.at[0], below, lo)),
        (has_above, has_below,
         rcopy(row_out.at[1], row_in.at[1], row_s.at[1], row_r.at[1], above, lo)),
    ]
    for side, (source, target, to) in enumerate(((east_out, west_in, right), (west_out, east_in, left))):
        s, r = col_s.at[side], col_r.at[side]
        halos += [
            (None, None, rcopy(source, target.at[pl.ds(2, rows)], s.at[0], r.at[0], la, to)),
            (has_below, has_above,
             rcopy(source.at[pl.ds(rows - 2, 2)], target.at[pl.ds(0, 2)], s.at[1], r.at[1], below, to)),
            (has_above, has_below,
             rcopy(source.at[pl.ds(0, 2)], target.at[pl.ds(rows + 2, 2)], s.at[2], r.at[2], above, to)),
        ]

    def guarded(guard, action):
        if guard is None:
            action()
        else:
            pl.when(guard)(action)

    for send, _, copy in halos:
        guarded(send, copy.start)
    gain_copies = []
    for d in range(1, nj):
        gain_copies.append(
            rcopy(gains, gain_in.at[lo], gain_s.at[d], gain_r.at[d], la, lax.rem(lo + d, nj))
        )
    for copy in gain_copies:
        copy.start()
    gain_in[lo] = gains[...]
    for _, arrive, copy in halos:
        guarded(arrive, copy.wait_recv)
    for side, (guard, base) in enumerate(((has_above, 0), (has_below, rows + 2))):
        @pl.when(guard)
        def _(side=side, base=base):
            for i in range(2):
                first_pad[base + i, 2 : cols + 2, :] = row_in[side, i]
                first_pad[base + i, 0:2, :] = west_in[base + i]
                first_pad[base + i, cols + 2 : wide, :] = east_in[base + i]
    for i in range(rows):
        first_pad[2 + i, 0:2, :] = west_in[2 + i]
        first_pad[2 + i, cols + 2 : wide, :] = east_in[2 + i]

    def a_copy(block, d):
        to = lax.rem(lo + d, nj)
        return rcopy(
            mine.at[span(to * part, part), lanes(block)], circle.at[lo, :, lanes(block)],
            a_s.at[block, d], a_r.at[block, d], la, to,
        )

    def z_copy(block, d):
        to = lax.rem(lo + d, nj)
        return rcopy(
            wide_out.at[pl.ds(to * rs, rs), :, lanes(block)],
            second_pad.at[pl.ds(2 + lo * rs, rs), :, lanes(block)],
            z_s.at[block, d], z_r.at[block, d], la, to,
        )

    def c_copy(t, a, b, source):
        return rcopy(
            sent_c.at[a, nj * t + b], spec_in.at[t, span(source * TILE, TILE), :],
            c_s.at[t], c_r.at[t], a, b,
        )

    def b_copy(t, a, b, la, lo):
        peer = a * nj + b
        return rcopy(
            spec_out.at[t, span(peer * TILE, TILE), :], got_c.at[la, nj * t + lo],
            b_s.at[t], b_r.at[t], a, b,
        )

    def keep_c(t):
        spec_in[t, span(me * TILE, TILE), :] = sent_c[la, nj * t + lo]

    def others(action):
        for d in range(1, nj):
            b = lax.rem(lo + d, nj)
            action(la * nj + b, la, b)

        def step(d, carry):
            a = lax.rem(la + d, nl)
            for b in range(nj):
                action(a * nj + b, a, b)
            return carry

        lax.fori_loop(1, nl, step, 0)

    def tiles(t, count, send, recv):
        block = spec_in.at[t, pl.ds(0, count * TILE), :]
        return rcopy(block, block, send.at[t], recv.at[t], below, right)

    def partners(t, action):
        owners = min(nj, units - nj * t)
        if owners == nj:
            action(total - 1)
        else:
            pl.when(lo < owners)(lambda: action(nl * owners - 1))
            pl.when(lo >= owners)(lambda: action(nl * owners))

    def own_unit(t, action):
        if nj * t + nj <= units:
            action()
        else:
            pl.when(nj * t + lo < units)(action)

    def real_unit(t, b, action):
        if nj * t + nj <= units:
            action()
        elif isinstance(b, int):
            if nj * t + b < units:
                action()
        else:
            pl.when(nj * t + b < units)(action)

    for block in range(blocks):
        sums = stencil_block(first_pad, taps1, lanes(block), rows, cols)
        for i in range(rows):
            mine[cols * i : cols * (i + 1), lanes(block)] = sums[i][:cols]
        for d in range(1, nj):
            a_copy(block, d).start()
        circle[lo, :, lanes(block)] = mine[span(lo * part, part), lanes(block)]

    for block in range(blocks):
        for d in range(1, nj):
            a_copy(block, d).wait_recv()
        values = circle[:, :, lanes(block)].reshape(nj * part, LANES)
        coeffs = mm3(fwd[0], fwd[1], values)
        sent_c[:, block * groups : (block + 1) * groups] = coeffs.reshape(nl, groups, TILE, LANES)
        for t in range(per):
            if (min(nj * (t + 1), units) - 1) // groups == block:
                others(lambda peer, a, b, t=t: real_unit(t, b, c_copy(t, a, b, me).start))
                own_unit(t, lambda t=t: keep_c(t))

    for copy in gain_copies:
        copy.wait_recv()
    width = gains.shape[1]
    for j in range(nj):
        gain_all[:, width * j : width * (j + 1)] = gain_in[j]
    loads[0].wait()
    loads[1].wait()

    def filter_unit(t):
        tiles(t, total - 1, c_s, c_r).wait_recv()
        unit = nj * t + lo
        block = unit // groups
        group = lax.rem(unit, groups)
        gain = gain_all[:, pl.ds(pl.multiple_of(block * LANES, LANES), LANES)]
        gain = jnp.concatenate([gain, gain], axis=1)
        for o in range(pair):
            data = jnp.concatenate(
                [spec_in[t, pl.ds(2 * o + ri, lat_count, stride=2 * pair), :] for ri in range(2)], axis=1
            )
            order = group * pair + o
            restored = mm_packed(pt[order], mm_packed(wt[order], data) * gain)
            for ri in range(2):
                spec_out[t, pl.ds(2 * o + ri, lat_count, stride=2 * pair), :] = (
                    restored[:, ri * LANES : (ri + 1) * LANES]
                )
        others(lambda peer, a, b: b_copy(t, a, b, la, lo).start())
        got_c[la, nj * t + lo] = spec_out[t, span(me * TILE, TILE), :]

    for t in range(per):
        own_unit(t, lambda t=t: filter_unit(t))

    taken = set()
    for block in range(blocks):
        for unit in range(block * groups, (block + 1) * groups):
            t = unit // nj
            if t not in taken:
                taken.add(t)
                partners(t, lambda count, t=t: tiles(t, count, b_s, b_r).wait_recv())
        coeffs = got_c[:, block * groups : (block + 1) * groups].reshape(nl * groups * TILE, LANES)
        values = circle[:, :, lanes(block)].reshape(nj * part, LANES)
        high, low = halves(values)
        rebuilt = mm3(back[0], back[1], coeffs) + (mm(pick[...], low) + mm(pick[...], high))
        wide_out[:, :, lanes(block)] = rebuilt.reshape(nj * rs, wide, LANES)
        for d in range(1, nj):
            z_copy(block, d).start()
        second_pad[pl.ds(2 + lo * rs, rs), :, lanes(block)] = wide_out[pl.ds(lo * rs, rs), :, lanes(block)]

    def row_copies(block):
        edge = second_pad.at[:, :, lanes(block)]
        return (
            (has_below, has_above,
             rcopy(edge.at[pl.ds(rows, 2)], edge.at[pl.ds(0, 2)], halo_s.at[block, 0], halo_r.at[block, 0], below, lo)),
            (has_above, has_below,
             rcopy(edge.at[pl.ds(2, 2)], edge.at[pl.ds(rows + 2, 2)], halo_s.at[block, 1], halo_r.at[block, 1], above, lo)),
        )

    for block in range(blocks):
        for d in range(1, nj):
            z_copy(block, d).wait_recv()
        for send, _, copy in row_copies(block):
            guarded(send, copy.start)
    for block in range(blocks):
        for _, arrive, copy in row_copies(block):
            guarded(arrive, copy.wait_recv)
        sums = stencil_block(second_pad, taps2, lanes(block), rows, cols)
        for i in range(rows):
            third[cols * i : cols * (i + 1), lanes(block)] = sums[i][:cols]

    loads[2].wait()
    loads[3].wait()
    state = third[...]
    average = jnp.mean(state, axis=-1, keepdims=True)
    centred = state - average
    spread = jnp.mean(centred * centred, axis=-1, keepdims=True)
    normed = (centred * lax.rsqrt(spread + 1e-05) * norm_gain[...].reshape(1, channels)).astype(bf16)
    active = jax.nn.gelu(mm(normed, up[...]), approximate=True).astype(bf16)
    third[...] = state + mm(active, down[...])
    for block in range(blocks):
        for i in range(rows):
            grid[block, pl.ds(i, cols, stride=rows), :] = third[cols * i : cols * (i + 1), lanes(block)]
        out_copy(block).start()

    for block in range(blocks):
        out_copy(block).wait()
    for send, _, copy in halos:
        guarded(send, copy.wait_send)
    for copy in gain_copies:
        copy.wait_send()
    for block in range(blocks):
        for d in range(1, nj):
            a_copy(block, d).wait_send()
            z_copy(block, d).wait_send()
        for send, _, copy in row_copies(block):
            guarded(send, copy.wait_send)

    for t in range(per):
        partners(t, lambda count, t=t: tiles(t, count, c_s, c_r).wait_send())
        own_unit(t, lambda t=t: tiles(t, total - 1, b_s, b_r).wait_send())


def fused(nl, nj, latent, conv_first, conv_second, filter_gains, norm_gain, up_weight, down_weight):
    rows, cols, channels = latent.shape
    modes, width = filter_gains.shape
    forward, back, pick, wt, pt = (jnp.asarray(t) for t in constant_tables(nl, nj, rows, cols, modes))
    rs = rows // nj
    wide = cols + 4
    blocks = channels // LANES
    total = nl * nj
    groups = modes // nl // (TILE // rs // 2)
    per = -(-groups * blocks // nj)
    vm = lambda *shape, kind=f32: pltpu.VMEM(shape, kind)
    dma = lambda *shape: pltpu.SemaphoreType.DMA(shape)
    here = pl.BlockSpec(memory_space=pltpu.VMEM)
    far = pl.BlockSpec(memory_space=pltpu.HBM)
    result = pl.pallas_call(
        functools.partial(block_kernel, nl, nj, rows),
        out_shape=jax.ShapeDtypeStruct((cols * rows, channels), f32),
        in_specs=[far] + [here] * 7 + [far] * 4,
        out_specs=far,
        scratch_shapes=[
            vm(blocks, cols * rows, LANES),
            vm(2, 2, cols, channels),
            vm(2, 2, cols, channels),
            vm(rows, 2, channels),
            vm(rows, 2, channels),
            vm(rows + 4, 2, channels),
            vm(rows + 4, 2, channels),
            vm(rows + 4, wide, channels),
            vm(rows * cols, channels),
            vm(nj, rs * cols, channels),
            vm(nl, per * nj, TILE, LANES),
            vm(per, total * TILE, LANES),
            vm(per, total * TILE, LANES),
            vm(nl, per * nj, TILE, LANES),
            vm(nj * rs, wide, channels),
            vm(rows + 4, wide, channels),
            vm(nj, modes, width),
            vm(modes, channels),
            vm(rows * cols, channels),
            vm(*up_weight.shape, kind=bf16),
            vm(*down_weight.shape, kind=bf16),
            vm(*wt.shape[1:], kind=bf16),
            vm(*pt.shape[1:], kind=bf16),
            dma(4), dma(blocks), dma(blocks),
            dma(2), dma(2), dma(2, 3), dma(2, 3), dma(nj), dma(nj),
            dma(blocks, nj), dma(blocks, nj), dma(per), dma(per), dma(per), dma(per),
            dma(blocks, nj), dma(blocks, nj), dma(blocks, 2), dma(blocks, 2),
        ],
        compiler_params=pltpu.CompilerParams(
            collective_id=0, has_side_effects=True, vmem_limit_bytes=60 * 1024 * 1024
        ),
        name="block",
    )(
        jnp.swapaxes(latent, 0, 1).reshape(cols * rows, channels), conv_first, conv_second,
        filter_gains, norm_gain, forward, back, pick, up_weight, down_weight, wt, pt,
    )
    return jnp.swapaxes(result.reshape(cols, rows, channels), 0, 1)


def fits(nl, nj, latent, filter_gains):
    rows, cols, channels = latent.shape
    modes = filter_gains.shape[0]
    if rows % nj or channels % LANES or modes % nl or nj < 2 or nl < 2:
        return False
    rs = rows // nj
    if TILE % (2 * rs) or (rs * cols) % TILE or (cols + 4) % TILE:
        return False
    if modes > LANES // 2 or rows * nl > LANES // 2:
        return False
    return (modes // nl) % (TILE // rs // 2) == 0


def body(latent, conv_first, conv_second, filter_gains, norm_gain, up_weight, down_weight):
    nl, nj = lax.axis_size("lat"), lax.axis_size("lon")
    arguments = (latent, conv_first, conv_second, filter_gains, norm_gain, up_weight, down_weight)
    if fits(nl, nj, latent, filter_gains):
        return fused(nl, nj, *arguments)
    return per_device(*arguments)


def solution(mesh):
    return jax.shard_map(
        body,
        mesh=mesh,
        in_specs=(P("lat", "lon", None), P(), P(), P(None, "lon"), P(), P(), P()),
        out_specs=P("lat", "lon", None),
        check_vma=False,
    )
```
